32 devices in a mesh: groups: 2 (over x), col: 16 (over z, y, core).
Axes of the slice: x: 2, y: 2, z: 4, core: 2. Of those that a mesh axis runs over, the one named last changes fastest.
Arguments:
- left_features: bfloat16 [32, 8, 8192], P(None, None, ('groups', 'col')), parts along dimension 2, may hold values from -3 to 3
- right_features: bfloat16 [32, 8, 8192], P(None, None, ('groups', 'col')), parts along dimension 2, may hold values from -3 to 3
- tile_offsets: int32 [32], P(('groups', 'col')), parts along dimension 0, may hold values from 0 to 3
- valid_mask: int32 [8, 8192], P(None, ('groups', 'col')), parts along dimension 1, may hold values 0 or 1
Outputs:
- disparity: float32 [8, 8192], P(None, ('groups', 'col')), parts along dimension 1
- final_volume: bfloat16 [192, 8, 8192], P(None, None, ('groups', 'col')), parts along dimension 2
The draws below stay inside these ranges and needn't reach their ends.
There are 2 independent parts, one for each index of `groups`. The reference program is written for one: setup_inputs(seed, part) draws one part's arguments, and reference() takes and returns one part's arrays. A program takes and returns all parts, laid end to end along the dimension named above; each array names one. Nothing has to cross between parts.
All inputs are finite; a program needn't handle non-finite values. No bound on the sum of `valid_mask` on one device may be relied on, other than what follows from the above.
Results may differ from the reference program's by a relative error of at most 0.001.
Values may be sent and summed in bfloat16 or wider, within the bound.
A program may use at most 64 MiB of HBM per device.

```python
import math
import jax
import jax.numpy as jnp
from jax import lax

C = 32
D = 192
W_DEV = 256
ROWS = 8
ITERS = 4
TILES = 16
COLS = 4096


def touch_ends(entries, rng, least, largest):
    place = [jax.random.randint(jax.random.fold_in(rng, axis), (), 0, length) for axis, length in enumerate(entries.shape)]
    longest = entries.shape.index(max(entries.shape))
    neighbour = place[:longest] + [(place[longest] + 1) % entries.shape[longest]] + place[longest + 1:]
    return entries.at[tuple(place)].set(least).at[tuple(neighbour)].set(largest)


def level_of(rng, dims, pieces, least, largest):
    def one(dim, shards_of):
        draws = jax.random.uniform(jax.random.fold_in(jax.random.fold_in(rng, 6), dim), (shards_of,), jnp.float32, least / len(pieces), largest / len(pieces))
        return jnp.repeat(jnp.exp(draws), dims[dim] // shards_of).reshape((-1,) + (1,) * (len(dims) - dim - 1))

    factor_of = one(*pieces[0])
    for cut in pieces[1:]:
        factor_of = factor_of * one(*cut)
    return factor_of


def centred(key, shape, width, most, shards=(), kind=jnp.bfloat16):
    loudness = level_of(key, shape, shards, -0.22, 0.18) if shards else 1.0
    array = jax.random.normal(key, shape, jnp.float32) * width * loudness
    return jnp.minimum(jnp.maximum(array, -most), most).astype(kind)


def setup_inputs(seed: int = 0, part: int = 0) -> dict:
    seeds = jax.random.split(jax.random.key(seed), 5)
    part_keys = jax.random.split(jax.random.fold_in(seeds[4], part), 5)
    left_features = centred(part_keys[0], (C, ROWS, COLS), 1.0, 3.0, ((2, 16),))
    right_features = centred(part_keys[1], (C, ROWS, COLS), 1.0, 3.0, ((2, 16),))
    tile_offsets = touch_ends(jax.random.randint(part_keys[2], (TILES,), 0, 4), jax.random.fold_in(part_keys[2], 1), 0, 3).astype(jnp.int32)
    valid_mask = touch_ends((jax.random.randint(part_keys[3], (ROWS, COLS), 0, 10) < 9).astype(jnp.int32), jax.random.fold_in(part_keys[3], 1), 0, 1)
    return dict(left_features=left_features, right_features=right_features, tile_offsets=tile_offsets, valid_mask=valid_mask)


FLOOR_COST = -4.0
NEIGHBOURS = tuple(((col_step, row_step) for col_step in (-1, 0, 1) for row_step in (-1, 0, 1)))

def affinity(padded, span, tile_rows, channels):
    center = padded[:, 1:1 + tile_rows, 1:1 + span]
    weights = []
    for col_step, row_step in NEIGHBOURS:
        beside = padded[:, 1 + row_step:1 + row_step + tile_rows, 1 + col_step:1 + col_step + span]
        distance = lax.optimization_barrier(jnp.sum((center - beside) ** 2, axis=0))
        weights.append(jnp.exp(-distance / (2.0 * channels)))
    stacked = jnp.stack(weights)
    return stacked / lax.optimization_barrier(jnp.sum(stacked, axis=0, keepdims=True))

def propagate(extended, weights, usable):
    center = extended[:, :, 1:-1]
    tile_rows = center.shape[1]
    span = center.shape[2]
    exponent = jnp.exp(center)
    total = lax.optimization_barrier(jnp.sum(exponent, axis=0))
    purity = center.shape[0] * lax.optimization_barrier(jnp.sum(exponent * exponent, axis=0)) / (total * total)
    gating = purity / (1.0 + purity)
    padded = jnp.pad(extended, ((0, 0), (1, 1), (0, 0)))
    pooled = jnp.zeros(center.shape, jnp.float32)
    for position, (col_step, row_step) in enumerate(NEIGHBOURS):
        beside = padded[:, 1 + row_step:1 + row_step + tile_rows, 1 + col_step:1 + col_step + span]
        pooled = pooled + weights[position][None] * beside
    lower = jnp.concatenate([pooled[:1], pooled[:-1]], axis=0)
    upper = jnp.concatenate([pooled[1:], pooled[-1:]], axis=0)
    smooth = 0.25 * lower + 0.5 * pooled + 0.25 * upper
    return usable[None] * (gating[None] * center + (1.0 - gating[None]) * smooth)

def reference(left_features, right_features, tile_offsets, valid_mask):
    left_float = left_features.astype(jnp.float32)
    right_padded = jnp.pad(right_features.astype(jnp.float32), ((0, 0), (0, 0), (D, 0)))

    def one_disparity(shift):
        moved = lax.dynamic_slice_in_dim(right_padded, (D - shift).astype(jnp.int32), COLS, 2)
        return lax.optimization_barrier(jnp.sum(left_float * moved, axis=0))
    corr = lax.map(one_disparity, jnp.arange(D, dtype=jnp.int32)) / math.sqrt(C)
    columns = jnp.arange(COLS, dtype=jnp.int32)
    tiles = columns // W_DEV
    reach = tile_offsets[tiles]
    shifts = jnp.arange(D, dtype=jnp.int32)
    allowed = columns[None, :] - shifts[:, None] >= (tiles - reach)[None, :] * W_DEV
    usable = valid_mask.astype(jnp.float32)
    volume = jnp.where(allowed[:, None, :], corr, FLOOR_COST) * usable[None]
    padded_guide = jnp.pad(left_float, ((0, 0), (1, 1), (1, 1)))
    weights = affinity(padded_guide, COLS, ROWS, C)
    for turn in range(ITERS):
        extended = jnp.pad(volume, ((0, 0), (0, 0), (1, 1)))
        volume = propagate(extended, weights, usable)
    exponent = jnp.exp(volume)
    probs = exponent / lax.optimization_barrier(jnp.sum(exponent, axis=0, keepdims=True))
    levels = (jnp.arange(D, dtype=jnp.float32) / D)[:, None, None]
    disparity = lax.optimization_barrier(jnp.sum(levels * probs, axis=0))
    return (disparity, volume.astype(jnp.bfloat16))
```

```python
import functools
import math

import jax
import jax.numpy as jnp
from jax import lax
from jax.experimental import pallas as pl
from jax.experimental.pallas import tpu as pltpu
from jax.sharding import PartitionSpec as P

D = 192
ITERS = 4
FLOOR_COST = -4.0
LANES = 128
SUB = 8
MESH = pl.DeviceIdType.MESH
STEPS = tuple((a, b) for a in (-1, 0, 1) for b in (-1, 0, 1))
PITCH = D + 8
GROUP = 32
PER = LANES // GROUP
BLOCKS = D // PER


def lroll(x, shift):
    shift = shift % x.shape[-1]
    return x if shift == 0 else pltpu.roll(x, shift, x.ndim - 1)


def sroll(x, shift):
    shift = shift % x.shape[-2]
    return x if shift == 0 else pltpu.roll(x, shift, x.ndim - 2)


def iota(shape, dim):
    return lax.broadcasted_iota(jnp.int32, shape, dim)


def distances(plane):
    right = lroll(plane, -1)
    others = (right, sroll(plane, -1), sroll(right, -1), sroll(lroll(plane, 1), -1))
    return tuple((plane - other) ** 2 for other in others) + (plane * plane,)


def affinity(sums, channels):
    across, down, down_right, down_left, norm = sums
    row = iota(across.shape, 0)
    first, last = row == 0, row == across.shape[0] - 1
    dist = {(1, 0): across, (-1, 0): lroll(across, 1)}
    for a, base in ((1, down_right), (0, down), (-1, down_left)):
        dist[a, 1] = jnp.where(last, norm, base)
        dist[-a, -1] = jnp.where(first, norm, sroll(lroll(base, a), 1))
    e = {k: jnp.exp(-d / (2.0 * channels)) for k, d in dist.items()}
    e[0, 0] = jnp.ones_like(across)
    total = sum(e[k] for k in STEPS)
    out = {k: e[k] / total for k in STEPS}
    for a in (-1, 0, 1):
        out[a, 1] = jnp.where(last, 0.0, out[a, 1])
        out[a, -1] = jnp.where(first, 0.0, out[a, -1])
    return out


def coefficients(weights, usable, s1, s2):
    purity = D * s2 / (s1 * s1)
    gating = purity / (1.0 + purity)
    part = 0.25 * usable * (1.0 - gating)
    return {k: sroll(weights[k] * part, k[1]) for k in STEPS}, usable * gating


def stencil(w, left, mid, right):
    z = {}
    for b in (-1, 0, 1):
        z[b] = w[-1, b] * left + w[0, b] * mid + w[1, b] * right
    return z[0] + (sroll(z[1], -1) + sroll(z[-1], 1))


def pack(planes):
    lane = iota((SUB, LANES), 1)
    place = lane % GROUP
    out = jnp.zeros((SUB, LANES), jnp.float32)
    for s, (head, tail) in enumerate(planes):
        mine = lane // GROUP == s
        out = jnp.where(mine & (place >= 4) & (place < 16), lroll(head, GROUP * s + 4), out)
        out = jnp.where(mine & (place >= 16) & (place < 28), lroll(tail, GROUP * s + 16 - 116), out)
    return out


def kernel(
    n, left_ref, right_ref, offs_ref, mask_ref, disp_ref, vol_ref,
    prev, lf, rs, t4, u, v, own, sent, from_left, from_right, st, w_ref, send_sem, recv_sem,
):
    channels = left_ref.shape[0]
    tile = left_ref.shape[2]
    me = lax.axis_index("col")
    has_left, has_right = me > 0, me < n - 1
    lane = iota((SUB, LANES), 1)

    barrier = pltpu.get_barrier_semaphore()

    @pl.when(has_left)
    def _():
        pl.semaphore_signal(barrier, inc=1, device_id={"col": me - 1}, device_id_type=MESH)

    @pl.when(has_right)
    def _():
        pl.semaphore_signal(barrier, inc=1, device_id={"col": me + 1}, device_id_type=MESH)

    pl.semaphore_wait(barrier, has_left.astype(jnp.int32) + has_right.astype(jnp.int32))

    def remote(src, dst, slot, to):
        return pltpu.make_async_remote_copy(
            src_ref=src, dst_ref=dst, send_sem=send_sem.at[slot], recv_sem=recv_sem.at[slot],
            device_id={"col": to}, device_id_type=MESH,
        )

    tile_copy = remote(right_ref, prev, 0, me + 1)
    strip_right = remote(sent, from_left, 1, me + 1)
    strip_left = remote(sent, from_right, 2, me - 1)

    @pl.when(has_right)
    def _():
        tile_copy.start()

    @pl.when(jnp.logical_not(has_left))
    def _():
        prev[...] = jnp.zeros(prev.shape, prev.dtype)
        from_left[...] = jnp.zeros(from_left.shape, jnp.float32)

    @pl.when(jnp.logical_not(has_right))
    def _():
        from_right[...] = jnp.zeros(from_right.shape, jnp.float32)

    usable = mask_ref[...].astype(jnp.float32)

    zero = jnp.zeros((SUB, tile), jnp.float32)

    def channel(c, sums):
        plane = left_ref[c].astype(jnp.float32)
        at = pl.ds(pl.multiple_of(c * SUB, SUB), SUB)
        lf[0, at, :] = plane[:, :LANES]
        lf[1, at, :] = plane[:, LANES:]
        return tuple(s + d for s, d in zip(sums, distances(plane)))

    weights = affinity(lax.fori_loop(0, channels, channel, (zero,) * 5), channels)
    for i, k in enumerate(STEPS):
        w_ref[i] = weights[k]

    for q in range(channels // PER):
        planes = [
            (lf[0, (q * PER + s) * SUB : (q * PER + s + 1) * SUB, :],
             lf[1, (q * PER + s) * SUB : (q * PER + s + 1) * SUB, :])
            for s in range(PER)
        ]
        own[BLOCKS + q] = pack(planes)
    mask_at = BLOCKS + channels // PER
    own[mask_at] = pack([(usable[:, :LANES], usable[:, LANES:])] * PER)
    for q in range(mask_at + 1, own.shape[0]):
        own[q] = jnp.zeros((SUB, LANES), jnp.float32)

    @pl.when(has_left)
    def _():
        tile_copy.wait_recv()

    def shifts(c, carry):
        at = pl.ds(pl.multiple_of(c * SUB, SUB), SUB)
        before = prev[c].astype(jnp.float32)
        mine = right_ref[c].astype(jnp.float32)
        parts = (before[:, :LANES], before[:, LANES:], mine[:, :LANES], mine[:, LANES:])
        for s in range(4):
            rolled = [lroll(p, -s) for p in parts]
            for t in range(4):
                value = rolled[t]
                if s and t < 3:
                    value = jnp.where(lane < LANES - s, value, rolled[t + 1])
                rs[s, t, at, :] = value
        return carry

    lax.fori_loop(0, channels, shifts, 0)

    depth = 8 * channels
    keep = (iota((depth, tile), 0) // channels == iota((depth, tile), 1) % 8).astype(jnp.bfloat16)
    rows_out = tile - 8 + D
    begin = tile - D + 1

    def row(y, carry):
        for t in range(4):
            block = jnp.concatenate(
                [rs[s, t, pl.ds(y, channels, stride=SUB), :] for s in range(4)], axis=0
            )
            t4[t * LANES : (t + 1) * LANES, :] = block.T
        lhs = jnp.concatenate(
            [t4[begin : begin + rows_out, :], t4[begin + 4 : begin + 4 + rows_out, :]], axis=1
        ).astype(jnp.bfloat16)
        l_row = jnp.concatenate(
            [lf[t, pl.ds(y, channels, stride=SUB), :] for t in range(2)], axis=1
        ).astype(jnp.bfloat16)
        rhs = jnp.concatenate([l_row] * 8, axis=0) * keep
        scores = jnp.dot(lhs, rhs, preferred_element_type=jnp.float32)
        for t in range(2):
            x = scores[LANES * t : LANES * t + D + LANES - 8, LANES * t : LANES * (t + 1)]
            for bit in (64, 32, 16, 8):
                size = x.shape[0] - bit
                on = (iota((size, LANES), 1) // bit) % 2 == 1
                x = jnp.where(on, x[bit:], x[:size])
            u[t, pl.ds(pl.multiple_of(y * PITCH, 8), D), :] = x
        return carry

    lax.fori_loop(0, SUB, row, 0)

    scale = 1.0 / math.sqrt(channels)
    reach = offs_ref[0] * tile
    half = [usable[:, :LANES], usable[:, LANES:]]
    none = jnp.zeros((SUB, LANES), jnp.float32)

    def first(b, sums):
        sums = list(sums)
        planes = []
        for s in range(PER):
            j = b * PER + s
            pair = []
            for t in range(2):
                corr = u[t, pl.ds(j, SUB, stride=PITCH), :] * scale
                allowed = lane + (t * LANES) >= (D - 1 - j) - reach
                value = jnp.where(allowed, corr, FLOOR_COST) * half[t]
                v[t, j] = value
                e = jnp.exp(value)
                sums[2 * t] += e
                sums[2 * t + 1] += e * e
                pair.append(value)
            planes.append(pair)
        own[b] = pack(planes)
        return tuple(sums)

    sums = lax.fori_loop(0, BLOCKS, first, (none,) * 4)

    place4 = (lane % GROUP) // 4
    for m in range(sent.shape[0]):
        out = own[4 * m]
        for s, (p, q) in ((1, (3, 0)), (2, (5, 2)), (3, (7, 4))):
            out = jnp.where((place4 == p) | (place4 == q), lroll(own[4 * m + s], 8 * s), out)
        sent[m] = out

    @pl.when(has_right)
    def _():
        strip_right.start()

    @pl.when(has_left)
    def _():
        strip_left.start()

    head_lane, tail_lane = lane == 0, lane == LANES - 1
    UN = PER

    def step(sums, last):
        coef = []
        for t in range(2):
            cols = slice(t * LANES, (t + 1) * LANES)
            coef.append(
                coefficients(
                    {k: w_ref[i, :, cols] for i, k in enumerate(STEPS)},
                    half[t], sums[2 * t], sums[2 * t + 1],
                )
            )

        def pooled(j):
            mid = (v[0, j], v[1, j])
            r = [lroll(m, 1) for m in mid]
            l = [lroll(m, -1) for m in mid]
            lefts = (r[0], jnp.where(head_lane, r[0], r[1]))
            rights = (jnp.where(tail_lane, l[1], l[0]), l[1])
            return [stencil(coef[t][0], lefts[t], mid[t], rights[t]) for t in range(2)], mid

        def finish(j, pair, sums, strip, s):
            sums = list(sums)
            if last:
                pair = list(pair)
                pair[0] = jnp.where(lane < 4, lroll(strip, -(GROUP * s + 4)), pair[0])
                pair[1] = jnp.where(lane >= LANES - 4, lroll(strip, 100 - GROUP * s), pair[1])
                vol_ref[D - 1 - j] = jnp.concatenate(pair, axis=1).astype(jnp.bfloat16)
                level = (D - 1 - j).astype(jnp.float32) * (1.0 / D)
            for t in range(2):
                if not last:
                    v[t, j] = pair[t]
                e = jnp.exp(pair[t])
                sums[2 * t] += e
                sums[2 * t + 1] += e * level if last else e * e
            return tuple(sums)

        def block(b, carry):
            p_prev, s_prev, v_prev, sums = carry
            for s in range(UN):
                j = b * UN + s
                p, mid = pooled(j)
                s_now = [p_prev[t] + p[t] for t in range(2)]
                new = [coef[t][1] * v_prev[t] + (s_prev[t] + s_now[t]) for t in range(2)]
                q = (s - 1) % PER
                strip = st[b - 1 if s == 0 else b] if last else None
                sums = finish(j - 1, new, sums, strip, q)
                p_prev, s_prev, v_prev = p, s_now, mid
            return p_prev, s_prev, v_prev, sums

        p0, mid0 = pooled(0)
        carry = (p0, [2.0 * p for p in p0], list(mid0), (none,) * 4)
        p_prev, s_prev, v_prev, acc = carry
        for s in range(1, UN):
            p, mid = pooled(s)
            s_now = [p_prev[t] + p[t] for t in range(2)]
            new = [coef[t][1] * v_prev[t] + (s_prev[t] + s_now[t]) for t in range(2)]
            acc = finish(jnp.int32(s - 1), new, acc, st[0] if last else None, s - 1)
            p_prev, s_prev, v_prev = p, s_now, list(mid)
        carry = (tuple(p_prev), tuple(s_prev), tuple(v_prev), acc)

        def loop(b, carry):
            p, s, m, acc = block(b, carry)
            return tuple(p), tuple(s), tuple(m), acc

        p_prev, s_prev, v_prev, acc = lax.fori_loop(1, D // UN, loop, carry)
        new = [
            coef[t][1] * v_prev[t] + (s_prev[t] + 2.0 * p_prev[t]) for t in range(2)
        ]
        return finish(jnp.int32(D - 1), new, acc, st[BLOCKS - 1] if last else None, PER - 1)

    sums = lax.fori_loop(0, ITERS - 1, lambda i, s: step(s, False), sums)

    @pl.when(has_left)
    def _():
        strip_right.wait_recv()

    @pl.when(has_right)
    def _():
        strip_left.wait_recv()

    place = lane % GROUP

    def joined(m, s):
        out = jnp.where(place < 4, lroll(from_left[m], -24 - 8 * s), own[4 * m + s])
        return jnp.where(place >= 28, lroll(from_right[m], 24 - 8 * s), out)

    def over_groups(x):
        x = x + lroll(x, GROUP)
        return x + lroll(x, 2 * GROUP)

    s1, s2 = none, none
    for m in range(BLOCKS // 4):
        for s in range(4):
            value = joined(m, s)
            st[4 * m + s] = value
            e = jnp.exp(value)
            s1, s2 = s1 + e, s2 + e * e
    strip_sums = (none,) * 5
    for q in range(channels // PER):
        at = BLOCKS + q
        strip_sums = [
            a + d for a, d in zip(strip_sums, distances(joined(at // 4, at % 4)))
        ]
    strip_weights = affinity([over_groups(x) for x in strip_sums], channels)
    strip_usable = joined(mask_at // 4, mask_at % 4)
    low, high = lane < GROUP, lane >= LANES - GROUP

    def strip_step(i, sums):
        s1, s2 = sums
        w, keep_own = coefficients(strip_weights, strip_usable, over_groups(s1), over_groups(s2))
        s1, s2 = none, none

        def pooled(value):
            p = stencil(w, lroll(value, 1), value, lroll(value, -1))
            return p, lroll(p, GROUP), lroll(p, -GROUP)

        value = st[0]
        p, up, down = pooled(value)
        lower = jnp.where(low, p, up)
        for b in range(BLOCKS):
            if b + 1 < BLOCKS:
                value_next = st[b + 1]
                p_next, up_next, down_next = pooled(value_next)
                upper = jnp.where(high, down_next, down)
            else:
                upper = jnp.where(high, p, down)
            new = keep_own * value + ((lower + upper) + 2.0 * p)
            st[b] = new
            e = jnp.exp(new)
            s1, s2 = s1 + e, s2 + e * e
            if b + 1 < BLOCKS:
                lower = jnp.where(low, up, up_next)
                value, p, up, down = value_next, p_next, up_next, down_next
        return s1, s2

    lax.fori_loop(0, ITERS, strip_step, (s1, s2))

    out = step(sums, True)
    for t in range(2):
        disp_ref[:, t * LANES : (t + 1) * LANES] = out[2 * t + 1] / out[2 * t]

    @pl.when(has_right)
    def _():
        tile_copy.wait_send()
        strip_right.wait_send()

    @pl.when(has_left)
    def _():
        strip_left.wait_send()


def on_device(n, left_features, right_features, tile_offsets, valid_mask):
    channels, rows, tile = left_features.shape
    vmem = pl.BlockSpec(memory_space=pltpu.VMEM)
    strips = -(-(BLOCKS + channels // PER + 1) // 4) * 4
    f32 = jnp.float32
    return pl.pallas_call(
        functools.partial(kernel, n),
        out_shape=(
            jax.ShapeDtypeStruct((rows, tile), f32),
            jax.ShapeDtypeStruct((D, rows, tile), jnp.bfloat16),
        ),
        in_specs=[vmem, vmem, pl.BlockSpec(memory_space=pltpu.SMEM), vmem],
        out_specs=(vmem, vmem),
        scratch_shapes=[
            pltpu.VMEM((channels, rows, tile), jnp.bfloat16),
            pltpu.VMEM((2, channels * SUB, LANES), f32),
            pltpu.VMEM((4, 4, channels * SUB, LANES), f32),
            pltpu.VMEM((2 * tile, LANES), f32),
            pltpu.VMEM((2, SUB * PITCH, LANES), f32),
            pltpu.VMEM((2, D, SUB, LANES), f32),
            pltpu.VMEM((strips, SUB, LANES), f32),
            pltpu.VMEM((strips // 4, SUB, LANES), f32),
            pltpu.VMEM((strips // 4, SUB, LANES), f32),
            pltpu.VMEM((strips // 4, SUB, LANES), f32),
            pltpu.VMEM((BLOCKS, SUB, LANES), f32),
            pltpu.VMEM((len(STEPS), SUB, tile), f32),
            pltpu.SemaphoreType.DMA((3,)),
            pltpu.SemaphoreType.DMA((3,)),
        ],
        compiler_params=pltpu.CompilerParams(collective_id=0, has_side_effects=True),
    )(left_features, right_features, tile_offsets, valid_mask)


def solution(mesh):
    return jax.shard_map(
        functools.partial(on_device, mesh.shape["col"]),
        mesh=mesh,
        in_specs=(
            P(None, None, ("groups", "col")),
            P(None, None, ("groups", "col")),
            P(("groups", "col")),
            P(None, ("groups", "col")),
        ),
        out_specs=(P(None, ("groups", "col")), P(None, None, ("groups", "col"))),
        check_vma=False,
    )
```

```python
import functools
import math

import jax
import jax.numpy as jnp
from jax import lax
from jax.experimental import pallas as pl
from jax.experimental.pallas import tpu as pltpu
from jax.sharding import PartitionSpec as P

D = 192
ITERS = 4
FLOOR_COST = -4.0
LANES = 128
SUB = 8
MESH = pl.DeviceIdType.MESH
STEPS = tuple((a, b) for a in (-1, 0, 1) for b in (-1, 0, 1))
PITCH = D + 8
GROUP = 32
PER = LANES // GROUP
BLOCKS = D // PER
LOG2E = math.log2(math.e)
FIRST_UNROLL = 4
UNROLL = 8
STRIP_UNROLL = 8
ROW_UNROLL = 2


def lroll(x, shift):
    shift = shift % x.shape[-1]
    return x if shift == 0 else pltpu.roll(x, shift, x.ndim - 1)


def sroll(x, shift):
    shift = shift % x.shape[-2]
    return x if shift == 0 else pltpu.roll(x, shift, x.ndim - 2)


def iota(shape, dim):
    return lax.broadcasted_iota(jnp.int32, shape, dim)


def distances(plane):
    right = lroll(plane, -1)
    others = (right, sroll(plane, -1), sroll(right, -1), sroll(lroll(plane, 1), -1))
    return tuple((plane - other) ** 2 for other in others) + (plane * plane,)


def affinity(sums, channels):
    across, down, down_right, down_left, norm = sums
    row = iota(across.shape, 0)
    first, last = row == 0, row == across.shape[0] - 1
    dist = {(1, 0): across, (-1, 0): lroll(across, 1)}
    for a, base in ((1, down_right), (0, down), (-1, down_left)):
        dist[a, 1] = jnp.where(last, norm, base)
        dist[-a, -1] = jnp.where(first, norm, sroll(lroll(base, a), 1))
    e = {k: jnp.exp(-d / (2.0 * channels)) for k, d in dist.items()}
    e[0, 0] = jnp.ones_like(across)
    total = sum(e[k] for k in STEPS)
    out = {k: e[k] / total for k in STEPS}
    for a in (-1, 0, 1):
        out[a, 1] = jnp.where(last, 0.0, out[a, 1])
        out[a, -1] = jnp.where(first, 0.0, out[a, -1])
    return out


def coefficients(weights, usable, s1, s2):
    purity = D * s2 / (s1 * s1)
    gating = purity / (1.0 + purity)
    part = 0.25 * usable * (1.0 - gating)
    return {k: lroll(weights[k] * part, k[0]) for k in STEPS}, usable * gating


def columns(w, above, mid, below):
    return [w[a, -1] * above + w[a, 0] * mid + w[a, 1] * below for a in (-1, 0, 1)]


def three(ref, s):
    at = (s + 1) * SUB
    return ref[at - 1 : at - 1 + SUB, :], ref[at : at + SUB, :], ref[at + 1 : at + 1 + SUB, :]


def pack(planes):
    lane = iota((SUB, LANES), 1)
    place = lane % GROUP
    out = jnp.zeros((SUB, LANES), jnp.float32)
    for s, (head, tail) in enumerate(planes):
        mine = lane // GROUP == s
        out = jnp.where(mine & (place >= 4) & (place < 16), lroll(head, GROUP * s + 4), out)
        out = jnp.where(mine & (place >= 16) & (place < 28), lroll(tail, GROUP * s + 16 - 116), out)
    return out


def kernel(
    n, left_ref, right_ref, offs_ref, mask_ref, disp_ref, vol_ref,
    prev, lf, rs, t4, u, v, own, sent, from_left, from_right, st, w_ref, send_sem, recv_sem,
):
    channels = left_ref.shape[0]
    tile = left_ref.shape[2]
    me = lax.axis_index("col")
    has_left, has_right = me > 0, me < n - 1
    lane = iota((SUB, LANES), 1)

    barrier = pltpu.get_barrier_semaphore()

    @pl.when(has_left)
    def _():
        pl.semaphore_signal(barrier, inc=1, device_id={"col": me - 1}, device_id_type=MESH)

    @pl.when(has_right)
    def _():
        pl.semaphore_signal(barrier, inc=1, device_id={"col": me + 1}, device_id_type=MESH)

    pl.semaphore_wait(barrier, has_left.astype(jnp.int32) + has_right.astype(jnp.int32))

    def remote(src, dst, slot, to):
        return pltpu.make_async_remote_copy(
            src_ref=src, dst_ref=dst, send_sem=send_sem.at[slot], recv_sem=recv_sem.at[slot],
            device_id={"col": to}, device_id_type=MESH,
        )

    tile_copy = remote(right_ref, prev, 0, me + 1)
    strip_right = remote(sent, from_left, 1, me + 1)
    strip_left = remote(sent, from_right, 2, me - 1)

    @pl.when(has_right)
    def _():
        tile_copy.start()

    @pl.when(jnp.logical_not(has_left))
    def _():
        prev[...] = jnp.zeros(prev.shape, prev.dtype)
        from_left[...] = jnp.zeros(from_left.shape, jnp.float32)

    @pl.when(jnp.logical_not(has_right))
    def _():
        from_right[...] = jnp.zeros(from_right.shape, jnp.float32)

    usable = mask_ref[...].astype(jnp.float32)

    zero = jnp.zeros((SUB, tile), jnp.float32)

    def channel(c, sums):
        plane = left_ref[c].astype(jnp.float32)
        at = pl.ds(pl.multiple_of(c * SUB, SUB), SUB)
        lf[0, at, :] = plane[:, :LANES]
        lf[1, at, :] = plane[:, LANES:]
        return tuple(s + d for s, d in zip(sums, distances(plane)))

    weights = affinity(lax.fori_loop(0, channels, channel, (zero,) * 5), channels)
    for i, k in enumerate(STEPS):
        w_ref[i] = weights[k]

    for q in range(channels // PER):
        planes = [
            (lf[0, (q * PER + s) * SUB : (q * PER + s + 1) * SUB, :],
             lf[1, (q * PER + s) * SUB : (q * PER + s + 1) * SUB, :])
            for s in range(PER)
        ]
        own[BLOCKS + q] = pack(planes)
    mask_at = BLOCKS + channels // PER
    own[mask_at] = pack([(usable[:, :LANES], usable[:, LANES:])] * PER)
    for q in range(mask_at + 1, own.shape[0]):
        own[q] = jnp.zeros((SUB, LANES), jnp.float32)

    @pl.when(has_left)
    def _():
        tile_copy.wait_recv()

    def shifts(c, carry):
        at = pl.ds(pl.multiple_of(c * SUB, SUB), SUB)
        before = prev[c].astype(jnp.float32)
        mine = right_ref[c].astype(jnp.float32)
        parts = (before[:, :LANES], before[:, LANES:], mine[:, :LANES], mine[:, LANES:])
        for s in range(4):
            rolled = [lroll(p, -s) for p in parts]
            for t in range(4):
                value = rolled[t]
                if s and t < 3:
                    value = jnp.where(lane < LANES - s, value, rolled[t + 1])
                rs[s, t, at, :] = value
        return carry

    lax.fori_loop(0, channels, shifts, 0)

    depth = 8 * channels
    keep = (iota((depth, tile), 0) // channels == iota((depth, tile), 1) % 8).astype(jnp.bfloat16)
    rows_out = tile - 8 + D
    begin = tile - D + 1

    def row(i, carry):
        for h in range(ROW_UNROLL):
            y = i * ROW_UNROLL + h
            for t in range(4):
                block = jnp.concatenate(
                    [rs[s, t, pl.ds(y, channels, stride=SUB), :] for s in range(4)], axis=0
                )
                t4[h, t * LANES : (t + 1) * LANES, :] = block.T
        for h in range(ROW_UNROLL):
            y = i * ROW_UNROLL + h
            lhs = jnp.concatenate(
                [t4[h, begin : begin + rows_out, :], t4[h, begin + 4 : begin + 4 + rows_out, :]],
                axis=1,
            ).astype(jnp.bfloat16)
            l_row = jnp.concatenate(
                [lf[t, pl.ds(y, channels, stride=SUB), :] for t in range(2)], axis=1
            ).astype(jnp.bfloat16)
            rhs = jnp.concatenate([l_row] * 8, axis=0) * keep
            scores = jnp.dot(lhs, rhs, preferred_element_type=jnp.float32)
            for t in range(2):
                x = scores[LANES * t : LANES * t + D + LANES - 8, LANES * t : LANES * (t + 1)]
                for bit in (64, 32, 16, 8):
                    size = x.shape[0] - bit
                    on = (iota((size, LANES), 1) // bit) % 2 == 1
                    x = jnp.where(on, x[bit:], x[:size])
                u[t, pl.ds(pl.multiple_of(y * PITCH, 8), D), :] = x
        return carry

    lax.fori_loop(0, SUB // ROW_UNROLL, row, 0)

    scale = LOG2E / math.sqrt(channels)
    reach = offs_ref[0] * tile
    half = [usable[:, :LANES], usable[:, LANES:]]
    none = jnp.zeros((SUB, LANES), jnp.float32)
    for t in range(2):
        v[t, :SUB, :] = none
        v[t, (D + 1) * SUB :, :] = none
    st[:SUB, :] = none
    st[(BLOCKS + 1) * SUB :, :] = none

    def first(i, sums):
        sums = list(sums)
        for h in range(FIRST_UNROLL):
            b = i * FIRST_UNROLL + h
            planes = []
            for s in range(PER):
                j = b * PER + s
                pair = []
                for t in range(2):
                    corr = u[t, pl.ds(j, SUB, stride=PITCH), :] * scale
                    allowed = lane >= (D - 1 - j) - reach - t * LANES
                    value = jnp.where(allowed, corr, FLOOR_COST * LOG2E) * half[t]
                    v[t, pl.ds(pl.multiple_of((j + 1) * SUB, SUB), SUB), :] = value
                    e = jnp.exp2(value)
                    sums[2 * t] += e
                    sums[2 * t + 1] += e * e
                    pair.append(value)
                planes.append(pair)
            own[b] = pack(planes)
        return tuple(sums)

    sums = lax.fori_loop(0, BLOCKS // FIRST_UNROLL, first, (none,) * 4)

    place4 = (lane % GROUP) // 4
    for m in range(sent.shape[0]):
        out = own[4 * m]
        for s, (p, q) in ((1, (3, 0)), (2, (5, 2)), (3, (7, 4))):
            out = jnp.where((place4 == p) | (place4 == q), lroll(own[4 * m + s], 8 * s), out)
        sent[m] = out

    @pl.when(has_right)
    def _():
        strip_right.start()

    @pl.when(has_left)
    def _():
        strip_left.start()

    head_lane, tail_lane = lane == 0, lane == LANES - 1

    def step(sums, last):
        wide = lambda a, b: jnp.concatenate([a, b], axis=1)
        w, keep_own = coefficients(
            {k: w_ref[i] for i, k in enumerate(STEPS)}, usable,
            wide(sums[0], sums[2]), wide(sums[1], sums[3]),
        )
        cut = lambda x, t: x[:, t * LANES : (t + 1) * LANES]
        w = [{k: cut(w[k], t) for k in STEPS} for t in range(2)]
        keep_own = [cut(keep_own, t) for t in range(2)]

        def pooled(refs, s):
            z, mid = [], []
            for t in range(2):
                rows = three(refs[t], s)
                mid.append(rows[1])
                z.append(columns(w[t], *rows))
            r = [lroll(z[t][0], 1) for t in range(2)]
            l = [lroll(z[t][2], -1) for t in range(2)]
            r[1] = jnp.where(head_lane, r[0], r[1])
            l[0] = jnp.where(tail_lane, l[1], l[0])
            return [z[t][1] + (r[t] + l[t]) for t in range(2)], mid

        def finish(b, s, pair, sums):
            j = b * UNROLL + s
            pair, sums = list(pair), list(sums)
            if last:
                group = s % PER
                row = pl.multiple_of((b * (UNROLL // PER) + s // PER + 1) * SUB, SUB)
                strip = st[pl.ds(row, SUB), :]
                pair[0] = jnp.where(lane < 4, lroll(strip, -(GROUP * group + 4)), pair[0])
                pair[1] = jnp.where(lane >= LANES - 4, lroll(strip, 100 - GROUP * group), pair[1])
                out = jnp.concatenate(pair, axis=1) * (1.0 / LOG2E)
                vol_ref[D - 1 - j] = out.astype(jnp.bfloat16)
                level = (D - 1 - j).astype(jnp.float32) * (1.0 / D)
            for t in range(2):
                if not last:
                    v[t, pl.ds(pl.multiple_of((j + 1) * SUB, SUB), SUB), :] = pair[t]
                e = jnp.exp2(pair[t])
                sums[2 * t] += e
                sums[2 * t + 1] += e * (level if last else e)
            return sums

        def advance(refs, b, s, carry):
            p_prev, s_prev, v_prev, acc = carry
            p, mid = pooled(refs, s)
            s_now = [p_prev[t] + p[t] for t in range(2)]
            new = [keep_own[t] * v_prev[t] + (s_prev[t] + s_now[t]) for t in range(2)]
            before = (b - 1, UNROLL - 1) if s == 0 else (b, s - 1)
            return p, s_now, mid, finish(*before, new, acc)

        def block_refs(b):
            at = pl.ds(pl.multiple_of(b * (UNROLL * SUB), SUB), (UNROLL + 2) * SUB)
            return [v.at[t, at, :] for t in range(2)]

        def loop(b, carry):
            p, s, m, acc = carry
            carry = list(p), list(s), list(m), list(acc)
            refs = block_refs(b)
            for k in range(UNROLL):
                carry = advance(refs, b, k, carry)
            return tuple(tuple(c) for c in carry)

        refs = block_refs(0)
        p, mid = pooled(refs, 0)
        carry = p, [2.0 * x for x in p], mid, [none] * 4
        for k in range(1, UNROLL):
            carry = advance(refs, jnp.int32(0), k, carry)
        carry = tuple(tuple(c) for c in carry)
        p_prev, s_prev, v_prev, acc = lax.fori_loop(1, D // UNROLL, loop, carry)
        new = [keep_own[t] * v_prev[t] + (s_prev[t] + 2.0 * p_prev[t]) for t in range(2)]
        return tuple(finish(jnp.int32(D // UNROLL - 1), UNROLL - 1, new, acc))

    sums = lax.fori_loop(0, ITERS - 1, lambda i, s: step(s, False), sums)

    @pl.when(has_left)
    def _():
        strip_right.wait_recv()

    @pl.when(has_right)
    def _():
        strip_left.wait_recv()

    place = lane % GROUP

    def joined(m, s):
        out = jnp.where(place < 4, lroll(from_left[m], -24 - 8 * s), own[4 * m + s])
        return jnp.where(place >= 28, lroll(from_right[m], 24 - 8 * s), out)

    def over_groups(x):
        x = x + lroll(x, GROUP)
        return x + lroll(x, 2 * GROUP)

    s1, s2 = none, none
    for m in range(BLOCKS // 4):
        for s in range(4):
            value = joined(m, s)
            st[(4 * m + s + 1) * SUB : (4 * m + s + 2) * SUB, :] = value
            e = jnp.exp2(value)
            s1, s2 = s1 + e, s2 + e * e
    strip_sums = (none,) * 5
    for q in range(channels // PER):
        at = BLOCKS + q
        strip_sums = [
            a + d for a, d in zip(strip_sums, distances(joined(at // 4, at % 4)))
        ]
    strip_weights = affinity([over_groups(x) for x in strip_sums], channels)
    strip_usable = joined(mask_at // 4, mask_at % 4)
    low, high = lane < GROUP, lane >= LANES - GROUP

    def strip_step(i, sums):
        w, keep_own = coefficients(
            strip_weights, strip_usable, over_groups(sums[0]), over_groups(sums[1])
        )

        def pooled(ref, s):
            rows = three(ref, s)
            z = columns(w, *rows)
            p = z[1] + (lroll(z[0], 1) + lroll(z[2], -1))
            return p, lroll(p, GROUP), lroll(p, -GROUP), rows[1]

        def finish(b, p, up, before, down, after, value, acc):
            lower, upper = jnp.where(low, before, up), jnp.where(high, after, down)
            new = keep_own * value + ((lower + upper) + 2.0 * p)
            st[pl.ds(pl.multiple_of((b + 1) * SUB, SUB), SUB), :] = new
            e = jnp.exp2(new)
            return acc[0] + e, acc[1] + e * e

        def advance(ref, b, s, carry):
            p, up, down, before, value, acc = carry
            p_now, up_now, down_now, value_now = pooled(ref, s)
            acc = finish(b * STRIP_UNROLL + s - 1, p, up, before, down, down_now, value, acc)
            return p_now, up_now, down_now, up, value_now, acc

        def block_ref(b):
            at = pl.ds(pl.multiple_of(b * (STRIP_UNROLL * SUB), SUB), (STRIP_UNROLL + 2) * SUB)
            return st.at[at, :]

        def loop(b, carry):
            ref = block_ref(b)
            for k in range(STRIP_UNROLL):
                carry = advance(ref, b, k, carry)
            return carry

        ref = block_ref(0)
        p, up, down, value = pooled(ref, 0)
        carry = p, up, down, p, value, (none, none)
        for k in range(1, STRIP_UNROLL):
            carry = advance(ref, jnp.int32(0), k, carry)
        p, up, down, before, value, acc = lax.fori_loop(1, BLOCKS // STRIP_UNROLL, loop, carry)
        return finish(jnp.int32(BLOCKS - 1), p, up, before, down, p, value, acc)

    lax.fori_loop(0, ITERS, strip_step, (s1, s2))

    out = step(sums, True)
    for t in range(2):
        disp_ref[:, t * LANES : (t + 1) * LANES] = out[2 * t + 1] / out[2 * t]

    @pl.when(has_right)
    def _():
        tile_copy.wait_send()
        strip_right.wait_send()

    @pl.when(has_left)
    def _():
        strip_left.wait_send()


def on_device(n, left_features, right_features, tile_offsets, valid_mask):
    channels, rows, tile = left_features.shape
    vmem = pl.BlockSpec(memory_space=pltpu.VMEM)
    strips = -(-(BLOCKS + channels // PER + 1) // 4) * 4
    f32 = jnp.float32
    return pl.pallas_call(
        functools.partial(kernel, n),
        out_shape=(
            jax.ShapeDtypeStruct((rows, tile), f32),
            jax.ShapeDtypeStruct((D, rows, tile), jnp.bfloat16),
        ),
        in_specs=[vmem, vmem, pl.BlockSpec(memory_space=pltpu.SMEM), vmem],
        out_specs=(vmem, vmem),
        scratch_shapes=[
            pltpu.VMEM((channels, rows, tile), jnp.bfloat16),
            pltpu.VMEM((2, channels * SUB, LANES), f32),
            pltpu.VMEM((4, 4, channels * SUB, LANES), f32),
            pltpu.VMEM((ROW_UNROLL, 2 * tile, LANES), f32),
            pltpu.VMEM((2, SUB * PITCH, LANES), f32),
            pltpu.VMEM((2, (D + 2) * SUB, LANES), f32),
            pltpu.VMEM((strips, SUB, LANES), f32),
            pltpu.VMEM((strips // 4, SUB, LANES), f32),
            pltpu.VMEM((strips // 4, SUB, LANES), f32),
            pltpu.VMEM((strips // 4, SUB, LANES), f32),
            pltpu.VMEM(((BLOCKS + 2) * SUB, LANES), f32),
            pltpu.VMEM((len(STEPS), SUB, tile), f32),
            pltpu.SemaphoreType.DMA((3,)),
            pltpu.SemaphoreType.DMA((3,)),
        ],
        compiler_params=pltpu.CompilerParams(collective_id=0, has_side_effects=True),
    )(left_features, right_features, tile_offsets, valid_mask)


def solution(mesh):
    return jax.shard_map(
        functools.partial(on_device, mesh.shape["col"]),
        mesh=mesh,
        in_specs=(
            P(None, None, ("groups", "col")),
            P(None, None, ("groups", "col")),
            P(("groups", "col")),
            P(None, ("groups", "col")),
        ),
        out_specs=(P(None, ("groups", "col")), P(None, None, ("groups", "col"))),
        check_vma=False,
    )
```

```python
import functools
import math

import jax
import jax.numpy as jnp
from jax import lax
from jax.experimental import pallas as pl
from jax.experimental.pallas import tpu as pltpu
from jax.sharding import PartitionSpec as P

D = 192
ITERS = 4
FLOOR_COST = -4.0
LANES = 128
SUB = 8
MESH = pl.DeviceIdType.MESH
STEPS = tuple((a, b) for a in (-1, 0, 1) for b in (-1, 0, 1))
PITCH = D + 8
GROUP = 32
PER = LANES // GROUP
BLOCKS = D // PER
LOG2E = math.log2(math.e)
FIRST_UNROLL = 48
UNROLL = 96
STRIP_UNROLL = 48
ROW_UNROLL = 4


def lroll(x, shift):
    shift = shift % x.shape[-1]
    return x if shift == 0 else pltpu.roll(x, shift, x.ndim - 1)


def sroll(x, shift):
    shift = shift % x.shape[-2]
    return x if shift == 0 else pltpu.roll(x, shift, x.ndim - 2)


def iota(shape, dim):
    return lax.broadcasted_iota(jnp.int32, shape, dim)


def distances(plane):
    right = lroll(plane, -1)
    others = (right, sroll(plane, -1), sroll(right, -1), sroll(lroll(plane, 1), -1))
    return tuple((plane - other) ** 2 for other in others) + (plane * plane,)


def affinity(sums, channels):
    across, down, down_right, down_left, norm = sums
    row = iota(across.shape, 0)
    first, last = row == 0, row == across.shape[0] - 1
    dist = {(1, 0): across, (-1, 0): lroll(across, 1)}
    for a, base in ((1, down_right), (0, down), (-1, down_left)):
        dist[a, 1] = jnp.where(last, norm, base)
        dist[-a, -1] = jnp.where(first, norm, sroll(lroll(base, a), 1))
    e = {k: jnp.exp(-d / (2.0 * channels)) for k, d in dist.items()}
    e[0, 0] = jnp.ones_like(across)
    total = sum(e[k] for k in STEPS)
    out = {k: e[k] / total for k in STEPS}
    for a in (-1, 0, 1):
        out[a, 1] = jnp.where(last, 0.0, out[a, 1])
        out[a, -1] = jnp.where(first, 0.0, out[a, -1])
    return out


def coefficients(weights, usable, s1, s2):
    purity = D * s2 / (s1 * s1)
    gating = purity / (1.0 + purity)
    part = 0.25 * usable * (1.0 - gating)
    return {k: lroll(weights[k] * part, k[0]) for k in STEPS}, usable * gating


def columns(w, above, mid, below):
    return [w[a, -1] * above + w[a, 0] * mid + w[a, 1] * below for a in (-1, 0, 1)]


def three(ref, s):
    at = (s + 1) * SUB
    return ref[at - 1 : at - 1 + SUB, :], ref[at : at + SUB, :], ref[at + 1 : at + 1 + SUB, :]


def pack(planes):
    lane = iota((SUB, LANES), 1)
    place = lane % GROUP
    out = jnp.zeros((SUB, LANES), jnp.float32)
    for s, (head, tail) in enumerate(planes):
        mine = lane // GROUP == s
        out = jnp.where(mine & (place >= 4) & (place < 16), lroll(head, GROUP * s + 4), out)
        out = jnp.where(mine & (place >= 16) & (place < 28), lroll(tail, GROUP * s + 16 - 116), out)
    return out


def kernel(
    n, left_ref, right_ref, offs_ref, mask_ref, disp_ref, vol_ref,
    prev, lf, rs, t4, u, v, own, sent, from_left, from_right, st, w_ref, send_sem, recv_sem,
):
    channels = left_ref.shape[0]
    tile = left_ref.shape[2]
    me = lax.axis_index("col")
    has_left, has_right = me > 0, me < n - 1
    lane = iota((SUB, LANES), 1)

    barrier = pltpu.get_barrier_semaphore()

    @pl.when(has_left)
    def _():
        pl.semaphore_signal(barrier, inc=1, device_id={"col": me - 1}, device_id_type=MESH)

    @pl.when(has_right)
    def _():
        pl.semaphore_signal(barrier, inc=1, device_id={"col": me + 1}, device_id_type=MESH)

    pl.semaphore_wait(barrier, has_left.astype(jnp.int32) + has_right.astype(jnp.int32))

    def remote(src, dst, slot, to):
        return pltpu.make_async_remote_copy(
            src_ref=src, dst_ref=dst, send_sem=send_sem.at[slot], recv_sem=recv_sem.at[slot],
            device_id={"col": to}, device_id_type=MESH,
        )

    tile_copy = remote(right_ref, prev, 0, me + 1)
    strip_right = remote(sent, from_left, 1, me + 1)
    strip_left = remote(sent, from_right, 2, me - 1)

    @pl.when(has_right)
    def _():
        tile_copy.start()

    @pl.when(jnp.logical_not(has_left))
    def _():
        prev[...] = jnp.zeros(prev.shape, prev.dtype)
        from_left[...] = jnp.zeros(from_left.shape, jnp.float32)

    @pl.when(jnp.logical_not(has_right))
    def _():
        from_right[...] = jnp.zeros(from_right.shape, jnp.float32)

    usable = mask_ref[...].astype(jnp.float32)

    zero = jnp.zeros((SUB, tile), jnp.float32)

    def channel(c, sums):
        plane = left_ref[c].astype(jnp.float32)
        at = pl.ds(pl.multiple_of(c * SUB, SUB), SUB)
        lf[0, at, :] = plane[:, :LANES]
        lf[1, at, :] = plane[:, LANES:]
        return tuple(s + d for s, d in zip(sums, distances(plane)))

    weights = affinity(lax.fori_loop(0, channels, channel, (zero,) * 5), channels)
    for i, k in enumerate(STEPS):
        w_ref[i] = weights[k]

    for q in range(channels // PER):
        planes = [
            (lf[0, (q * PER + s) * SUB : (q * PER + s + 1) * SUB, :],
             lf[1, (q * PER + s) * SUB : (q * PER + s + 1) * SUB, :])
            for s in range(PER)
        ]
        own[BLOCKS + q] = pack(planes)
    mask_at = BLOCKS + channels // PER
    own[mask_at] = pack([(usable[:, :LANES], usable[:, LANES:])] * PER)
    for q in range(mask_at + 1, own.shape[0]):
        own[q] = jnp.zeros((SUB, LANES), jnp.float32)

    @pl.when(has_left)
    def _():
        tile_copy.wait_recv()

    def shifts(c, carry):
        at = pl.ds(pl.multiple_of(c * SUB, SUB), SUB)
        before = prev[c].astype(jnp.float32)
        mine = right_ref[c].astype(jnp.float32)
        parts = (before[:, :LANES], before[:, LANES:], mine[:, :LANES], mine[:, LANES:])
        for s in range(4):
            rolled = [lroll(p, -s) for p in parts]
            for t in range(4):
                value = rolled[t]
                if s and t < 3:
                    value = jnp.where(lane < LANES - s, value, rolled[t + 1])
                rs[s, t, at, :] = value
        return carry

    lax.fori_loop(0, channels, shifts, 0)

    depth = 8 * channels
    keep = (iota((depth, tile), 0) // channels == iota((depth, tile), 1) % 8).astype(jnp.bfloat16)
    rows_out = tile - 8 + D
    begin = tile - D + 1

    def row(i, carry):
        for h in range(ROW_UNROLL):
            y = i * ROW_UNROLL + h
            for t in range(4):
                block = jnp.concatenate(
                    [rs[s, t, pl.ds(y, channels, stride=SUB), :] for s in range(4)], axis=0
                )
                t4[h, t * LANES : (t + 1) * LANES, :] = block.T
        for h in range(ROW_UNROLL):
            y = i * ROW_UNROLL + h
            lhs = jnp.concatenate(
                [t4[h, begin : begin + rows_out, :], t4[h, begin + 4 : begin + 4 + rows_out, :]],
                axis=1,
            ).astype(jnp.bfloat16)
            l_row = jnp.concatenate(
                [lf[t, pl.ds(y, channels, stride=SUB), :] for t in range(2)], axis=1
            ).astype(jnp.bfloat16)
            rhs = jnp.concatenate([l_row] * 8, axis=0) * keep
            scores = jnp.dot(lhs, rhs, preferred_element_type=jnp.float32)
            for t in range(2):
                x = scores[LANES * t : LANES * t + D + LANES - 8, LANES * t : LANES * (t + 1)]
                for bit in (64, 32, 16, 8):
                    size = x.shape[0] - bit
                    on = (iota((size, LANES), 1) // bit) % 2 == 1
                    x = jnp.where(on, x[bit:], x[:size])
                u[t, pl.ds(pl.multiple_of(y * PITCH, 8), D), :] = x
        return carry

    lax.fori_loop(0, SUB // ROW_UNROLL, row, 0)

    scale = LOG2E / math.sqrt(channels)
    reach = offs_ref[0] * tile
    half = [usable[:, :LANES], usable[:, LANES:]]
    none = jnp.zeros((SUB, LANES), jnp.float32)
    for t in range(2):
        v[t, :SUB, :] = none
        v[t, (D + 1) * SUB :, :] = none
    st[:SUB, :] = none
    st[(BLOCKS + 1) * SUB :, :] = none

    def first(i, sums):
        sums = list(sums)
        for h in range(FIRST_UNROLL):
            b = i * FIRST_UNROLL + h
            planes = []
            for s in range(PER):
                j = b * PER + s
                pair = []
                for t in range(2):
                    corr = u[t, pl.ds(j, SUB, stride=PITCH), :] * scale
                    allowed = lane >= (D - 1 - j) - reach - t * LANES
                    value = jnp.where(allowed, corr, FLOOR_COST * LOG2E) * half[t]
                    v[t, pl.ds(pl.multiple_of((j + 1) * SUB, SUB), SUB), :] = value
                    e = jnp.exp2(value)
                    sums[2 * t] += e
                    sums[2 * t + 1] += e * e
                    pair.append(value)
                planes.append(pair)
            own[b] = pack(planes)
        return tuple(sums)

    sums = lax.fori_loop(0, BLOCKS // FIRST_UNROLL, first, (none,) * 4)

    place4 = (lane % GROUP) // 4
    for m in range(sent.shape[0]):
        out = own[4 * m]
        for s, (p, q) in ((1, (3, 0)), (2, (5, 2)), (3, (7, 4))):
            out = jnp.where((place4 == p) | (place4 == q), lroll(own[4 * m + s], 8 * s), out)
        sent[m] = out

    @pl.when(has_right)
    def _():
        strip_right.start()

    @pl.when(has_left)
    def _():
        strip_left.start()

    head_lane, tail_lane = lane == 0, lane == LANES - 1

    def step(sums, last):
        wide = lambda a, b: jnp.concatenate([a, b], axis=1)
        w, keep_own = coefficients(
            {k: w_ref[i] for i, k in enumerate(STEPS)}, usable,
            wide(sums[0], sums[2]), wide(sums[1], sums[3]),
        )
        cut = lambda x, t: x[:, t * LANES : (t + 1) * LANES]
        w = [{k: cut(w[k], t) for k in STEPS} for t in range(2)]
        keep_own = [cut(keep_own, t) for t in range(2)]

        def pooled(refs, s):
            z, mid = [], []
            for t in range(2):
                rows = three(refs[t], s)
                mid.append(rows[1])
                z.append(columns(w[t], *rows))
            r = [lroll(z[t][0], 1) for t in range(2)]
            l = [lroll(z[t][2], -1) for t in range(2)]
            r[1] = jnp.where(head_lane, r[0], r[1])
            l[0] = jnp.where(tail_lane, l[1], l[0])
            return [z[t][1] + (r[t] + l[t]) for t in range(2)], mid

        def finish(b, s, pair, sums):
            j = b * UNROLL + s
            pair, sums = list(pair), list(sums)
            if last:
                group = s % PER
                row = pl.multiple_of((b * (UNROLL // PER) + s // PER + 1) * SUB, SUB)
                strip = st[pl.ds(row, SUB), :]
                pair[0] = jnp.where(lane < 4, lroll(strip, -(GROUP * group + 4)), pair[0])
                pair[1] = jnp.where(lane >= LANES - 4, lroll(strip, 100 - GROUP * group), pair[1])
                out = jnp.concatenate(pair, axis=1) * (1.0 / LOG2E)
                vol_ref[D - 1 - j] = out.astype(jnp.bfloat16)
                level = (D - 1 - j).astype(jnp.float32) * (1.0 / D)
            for t in range(2):
                if not last:
                    v[t, pl.ds(pl.multiple_of((j + 1) * SUB, SUB), SUB), :] = pair[t]
                e = jnp.exp2(pair[t])
                sums[2 * t] += e
                sums[2 * t + 1] += e * (level if last else e)
            return sums

        def advance(refs, b, s, carry):
            p_prev, s_prev, v_prev, acc = carry
            p, mid = pooled(refs, s)
            s_now = [p_prev[t] + p[t] for t in range(2)]
            new = [keep_own[t] * v_prev[t] + (s_prev[t] + s_now[t]) for t in range(2)]
            before = (b - 1, UNROLL - 1) if s == 0 else (b, s - 1)
            return p, s_now, mid, finish(*before, new, acc)

        def block_refs(b):
            at = pl.ds(pl.multiple_of(b * (UNROLL * SUB), SUB), (UNROLL + 2) * SUB)
            return [v.at[t, at, :] for t in range(2)]

        def loop(b, carry):
            p, s, m, acc = carry
            carry = list(p), list(s), list(m), list(acc)
            refs = block_refs(b)
            for k in range(UNROLL):
                carry = advance(refs, b, k, carry)
            return tuple(tuple(c) for c in carry)

        refs = block_refs(0)
        p, mid = pooled(refs, 0)
        carry = p, [2.0 * x for x in p], mid, [none] * 4
        for k in range(1, UNROLL):
            carry = advance(refs, jnp.int32(0), k, carry)
        carry = tuple(tuple(c) for c in carry)
        p_prev, s_prev, v_prev, acc = lax.fori_loop(1, D // UNROLL, loop, carry)
        new = [keep_own[t] * v_prev[t] + (s_prev[t] + 2.0 * p_prev[t]) for t in range(2)]
        return tuple(finish(jnp.int32(D // UNROLL - 1), UNROLL - 1, new, acc))

    sums = lax.fori_loop(0, ITERS - 1, lambda i, s: step(s, False), sums)

    @pl.when(has_left)
    def _():
        strip_right.wait_recv()

    @pl.when(has_right)
    def _():
        strip_left.wait_recv()

    place = lane % GROUP

    def joined(m, s):
        out = jnp.where(place < 4, lroll(from_left[m], -24 - 8 * s), own[4 * m + s])
        return jnp.where(place >= 28, lroll(from_right[m], 24 - 8 * s), out)

    def over_groups(x):
        x = x + lroll(x, GROUP)
        return x + lroll(x, 2 * GROUP)

    s1, s2 = none, none
    for m in range(BLOCKS // 4):
        for s in range(4):
            value = joined(m, s)
            st[(4 * m + s + 1) * SUB : (4 * m + s + 2) * SUB, :] = value
            e = jnp.exp2(value)
            s1, s2 = s1 + e, s2 + e * e
    strip_sums = (none,) * 5
    for q in range(channels // PER):
        at = BLOCKS + q
        strip_sums = [
            a + d for a, d in zip(strip_sums, distances(joined(at // 4, at % 4)))
        ]
    strip_weights = affinity([over_groups(x) for x in strip_sums], channels)
    strip_usable = joined(mask_at // 4, mask_at % 4)
    low, high = lane < GROUP, lane >= LANES - GROUP

    def strip_step(i, sums):
        w, keep_own = coefficients(
            strip_weights, strip_usable, over_groups(sums[0]), over_groups(sums[1])
        )

        def pooled(ref, s):
            rows = three(ref, s)
            z = columns(w, *rows)
            p = z[1] + (lroll(z[0], 1) + lroll(z[2], -1))
            return p, lroll(p, GROUP), lroll(p, -GROUP), rows[1]

        def finish(b, p, up, before, down, after, value, acc):
            lower, upper = jnp.where(low, before, up), jnp.where(high, after, down)
            new = keep_own * value + ((lower + upper) + 2.0 * p)
            st[pl.ds(pl.multiple_of((b + 1) * SUB, SUB), SUB), :] = new
            e = jnp.exp2(new)
            return acc[0] + e, acc[1] + e * e

        def advance(ref, b, s, carry):
            p, up, down, before, value, acc = carry
            p_now, up_now, down_now, value_now = pooled(ref, s)
            acc = finish(b * STRIP_UNROLL + s - 1, p, up, before, down, down_now, value, acc)
            return p_now, up_now, down_now, up, value_now, acc

        def block_ref(b):
            at = pl.ds(pl.multiple_of(b * (STRIP_UNROLL * SUB), SUB), (STRIP_UNROLL + 2) * SUB)
            return st.at[at, :]

        def loop(b, carry):
            ref = block_ref(b)
            for k in range(STRIP_UNROLL):
                carry = advance(ref, b, k, carry)
            return carry

        ref = block_ref(0)
        p, up, down, value = pooled(ref, 0)
        carry = p, up, down, p, value, (none, none)
        for k in range(1, STRIP_UNROLL):
            carry = advance(ref, jnp.int32(0), k, carry)
        p, up, down, before, value, acc = lax.fori_loop(1, BLOCKS // STRIP_UNROLL, loop, carry)
        return finish(jnp.int32(BLOCKS - 1), p, up, before, down, p, value, acc)

    lax.fori_loop(0, ITERS, strip_step, (s1, s2))

    out = step(sums, True)
    for t in range(2):
        disp_ref[:, t * LANES : (t + 1) * LANES] = out[2 * t + 1] / out[2 * t]

    @pl.when(has_right)
    def _():
        tile_copy.wait_send()
        strip_right.wait_send()

    @pl.when(has_left)
    def _():
        strip_left.wait_send()


def on_device(n, left_features, right_features, tile_offsets, valid_mask):
    channels, rows, tile = left_features.shape
    vmem = pl.BlockSpec(memory_space=pltpu.VMEM)
    strips = -(-(BLOCKS + channels // PER + 1) // 4) * 4
    f32 = jnp.float32
    return pl.pallas_call(
        functools.partial(kernel, n),
        out_shape=(
            jax.ShapeDtypeStruct((rows, tile), f32),
            jax.ShapeDtypeStruct((D, rows, tile), jnp.bfloat16),
        ),
        in_specs=[vmem, vmem, pl.BlockSpec(memory_space=pltpu.SMEM), vmem],
        out_specs=(vmem, vmem),
        scratch_shapes=[
            pltpu.VMEM((channels, rows, tile), jnp.bfloat16),
            pltpu.VMEM((2, channels * SUB, LANES), f32),
            pltpu.VMEM((4, 4, channels * SUB, LANES), f32),
            pltpu.VMEM((ROW_UNROLL, 2 * tile, LANES), f32),
            pltpu.VMEM((2, SUB * PITCH, LANES), f32),
            pltpu.VMEM((2, (D + 2) * SUB, LANES), f32),
            pltpu.VMEM((strips, SUB, LANES), f32),
            pltpu.VMEM((strips // 4, SUB, LANES), f32),
            pltpu.VMEM((strips // 4, SUB, LANES), f32),
            pltpu.VMEM((strips // 4, SUB, LANES), f32),
            pltpu.VMEM(((BLOCKS + 2) * SUB, LANES), f32),
            pltpu.VMEM((len(STEPS), SUB, tile), f32),
            pltpu.SemaphoreType.DMA((3,)),
            pltpu.SemaphoreType.DMA((3,)),
        ],
        compiler_params=pltpu.CompilerParams(collective_id=0, has_side_effects=True),
    )(left_features, right_features, tile_offsets, valid_mask)


def solution(mesh):
    return jax.shard_map(
        functools.partial(on_device, mesh.shape["col"]),
        mesh=mesh,
        in_specs=(
            P(None, None, ("groups", "col")),
            P(None, None, ("groups", "col")),
            P(("groups", "col")),
            P(None, ("groups", "col")),
        ),
        out_specs=(P(None, ("groups", "col")), P(None, None, ("groups", "col"))),
        check_vma=False,
    )
```

```python
import functools
import math

import jax
import jax.numpy as jnp
from jax import lax
from jax.experimental import pallas as pl
from jax.experimental.pallas import tpu as pltpu
from jax.sharding import PartitionSpec as P

D = 192
ITERS = 4
FLOOR_COST = -4.0
LANES = 128
SUB = 8
MESH = pl.DeviceIdType.MESH
STEPS = tuple((a, b) for a in (-1, 0, 1) for b in (-1, 0, 1))
PITCH = D + 8
GROUP = 32
PER = LANES // GROUP
BLOCKS = D // PER
LOG2E = math.log2(math.e)
FIRST_UNROLL = 48
UNROLL = 96
STRIP_UNROLL = 48
ROW_UNROLL = 4
CHANNEL_UNROLL = 8
VMEM_LIMIT = 24 * 1024 * 1024


def lroll(x, shift):
    shift = shift % x.shape[-1]
    return x if shift == 0 else pltpu.roll(x, shift, x.ndim - 1)


def sroll(x, shift):
    shift = shift % x.shape[-2]
    return x if shift == 0 else pltpu.roll(x, shift, x.ndim - 2)


def iota(shape, dim):
    return lax.broadcasted_iota(jnp.int32, shape, dim)


def distances(plane):
    right = lroll(plane, -1)
    others = (right, sroll(plane, -1), sroll(right, -1), sroll(lroll(plane, 1), -1))
    return tuple((plane - other) ** 2 for other in others) + (plane * plane,)


def affinity(sums, channels):
    across, down, down_right, down_left, norm = sums
    row = iota(across.shape, 0)
    first, last = row == 0, row == across.shape[0] - 1
    dist = {(1, 0): across, (-1, 0): lroll(across, 1)}
    for a, base in ((1, down_right), (0, down), (-1, down_left)):
        dist[a, 1] = jnp.where(last, norm, base)
        dist[-a, -1] = jnp.where(first, norm, sroll(lroll(base, a), 1))
    e = {k: jnp.exp(-d / (2.0 * channels)) for k, d in dist.items()}
    e[0, 0] = jnp.ones_like(across)
    total = sum(e[k] for k in STEPS)
    out = {k: e[k] / total for k in STEPS}
    for a in (-1, 0, 1):
        out[a, 1] = jnp.where(last, 0.0, out[a, 1])
        out[a, -1] = jnp.where(first, 0.0, out[a, -1])
    return out


def coefficients(weights, usable, s1, s2):
    purity = D * s2 / (s1 * s1)
    gating = purity / (1.0 + purity)
    part = 0.25 * usable * (1.0 - gating)
    return {k: lroll(weights[k] * part, k[0]) for k in STEPS}, usable * gating


def columns(w, above, mid, below):
    return [w[a, -1] * above + w[a, 0] * mid + w[a, 1] * below for a in (-1, 0, 1)]


def three(ref, s):
    at = (s + 1) * SUB
    return ref[at - 1 : at - 1 + SUB, :], ref[at : at + SUB, :], ref[at + 1 : at + 1 + SUB, :]


def pack(planes):
    lane = iota((SUB, LANES), 1)
    place = lane % GROUP
    out = jnp.zeros((SUB, LANES), jnp.float32)
    for s, (head, tail) in enumerate(planes):
        mine = lane // GROUP == s
        out = jnp.where(mine & (place >= 4) & (place < 16), lroll(head, GROUP * s + 4), out)
        out = jnp.where(mine & (place >= 16) & (place < 28), lroll(tail, GROUP * s + 16 - 116), out)
    return out


def step(v, st, w_ref, usable, vol_ref, sums):
    last = vol_ref is not None
    lane = iota((SUB, LANES), 1)
    head_lane, tail_lane = lane == 0, lane == LANES - 1
    none = jnp.zeros((SUB, LANES), jnp.float32)
    wide = lambda a, b: jnp.concatenate([a, b], axis=1)
    w, keep_own = coefficients(
        {k: w_ref[i] for i, k in enumerate(STEPS)}, usable,
        wide(sums[0], sums[2]), wide(sums[1], sums[3]),
    )
    cut = lambda x, t: x[:, t * LANES : (t + 1) * LANES]
    w = [{k: cut(w[k], t) for k in STEPS} for t in range(2)]
    keep_own = [cut(keep_own, t) for t in range(2)]

    def pooled(refs, s):
        z, mid = [], []
        for t in range(2):
            rows = three(refs[t], s)
            mid.append(rows[1])
            z.append(columns(w[t], *rows))
        r = [lroll(z[t][0], 1) for t in range(2)]
        l = [lroll(z[t][2], -1) for t in range(2)]
        r[1] = jnp.where(head_lane, r[0], r[1])
        l[0] = jnp.where(tail_lane, l[1], l[0])
        return [z[t][1] + (r[t] + l[t]) for t in range(2)], mid

    def finish(b, s, pair, sums):
        j = b * UNROLL + s
        pair, sums = list(pair), list(sums)
        if last:
            group = s % PER
            row = pl.multiple_of((b * (UNROLL // PER) + s // PER + 1) * SUB, SUB)
            strip = st[pl.ds(row, SUB), :]
            pair[0] = jnp.where(lane < 4, lroll(strip, -(GROUP * group + 4)), pair[0])
            pair[1] = jnp.where(lane >= LANES - 4, lroll(strip, 100 - GROUP * group), pair[1])
            out = jnp.concatenate(pair, axis=1) * (1.0 / LOG2E)
            vol_ref[D - 1 - j] = out.astype(jnp.bfloat16)
            level = (D - 1 - j).astype(jnp.float32) * (1.0 / D)
        for t in range(2):
            if not last:
                v[t, pl.ds(pl.multiple_of((j + 1) * SUB, SUB), SUB), :] = pair[t]
            e = jnp.exp2(pair[t])
            sums[2 * t] += e
            sums[2 * t + 1] += e * (level if last else e)
        return sums

    def advance(refs, b, s, carry):
        p_prev, s_prev, v_prev, acc = carry
        p, mid = pooled(refs, s)
        s_now = [p_prev[t] + p[t] for t in range(2)]
        new = [keep_own[t] * v_prev[t] + (s_prev[t] + s_now[t]) for t in range(2)]
        before = (b - 1, UNROLL - 1) if s == 0 else (b, s - 1)
        return p, s_now, mid, finish(*before, new, acc)

    def block_refs(b):
        at = pl.ds(pl.multiple_of(b * (UNROLL * SUB), SUB), (UNROLL + 2) * SUB)
        return [v.at[t, at, :] for t in range(2)]

    def loop(b, carry):
        p, s, m, acc = carry
        carry = list(p), list(s), list(m), list(acc)
        refs = block_refs(b)
        for k in range(UNROLL):
            carry = advance(refs, b, k, carry)
        return tuple(tuple(c) for c in carry)

    refs = block_refs(0)
    p, mid = pooled(refs, 0)
    carry = p, [2.0 * x for x in p], mid, [none] * 4
    for k in range(1, UNROLL):
        carry = advance(refs, jnp.int32(0), k, carry)
    carry = tuple(tuple(c) for c in carry)
    p_prev, s_prev, v_prev, acc = lax.fori_loop(1, D // UNROLL, loop, carry)
    new = [keep_own[t] * v_prev[t] + (s_prev[t] + 2.0 * p_prev[t]) for t in range(2)]
    return tuple(finish(jnp.int32(D // UNROLL - 1), UNROLL - 1, new, acc))


def kernel(
    n, left_ref, right_ref, offs_ref, mask_ref, v, st, w_ref, sums_ref,
    prev, lf, rs, t4, u, own, sent, from_left, from_right, send_sem, recv_sem,
):
    channels = left_ref.shape[0]
    tile = left_ref.shape[2]
    me = lax.axis_index("col")
    has_left, has_right = me > 0, me < n - 1
    lane = iota((SUB, LANES), 1)

    barrier = pltpu.get_barrier_semaphore()

    @pl.when(has_left)
    def _():
        pl.semaphore_signal(barrier, inc=1, device_id={"col": me - 1}, device_id_type=MESH)

    @pl.when(has_right)
    def _():
        pl.semaphore_signal(barrier, inc=1, device_id={"col": me + 1}, device_id_type=MESH)

    pl.semaphore_wait(barrier, has_left.astype(jnp.int32) + has_right.astype(jnp.int32))

    def remote(src, dst, slot, to):
        return pltpu.make_async_remote_copy(
            src_ref=src, dst_ref=dst, send_sem=send_sem.at[slot], recv_sem=recv_sem.at[slot],
            device_id={"col": to}, device_id_type=MESH,
        )

    tile_copy = remote(right_ref, prev, 0, me + 1)
    strip_right = remote(sent, from_left, 1, me + 1)
    strip_left = remote(sent, from_right, 2, me - 1)

    @pl.when(has_right)
    def _():
        tile_copy.start()

    @pl.when(jnp.logical_not(has_left))
    def _():
        prev[...] = jnp.zeros(prev.shape, prev.dtype)
        from_left[...] = jnp.zeros(from_left.shape, jnp.float32)

    @pl.when(jnp.logical_not(has_right))
    def _():
        from_right[...] = jnp.zeros(from_right.shape, jnp.float32)

    usable = mask_ref[...].astype(jnp.float32)

    zero = jnp.zeros((SUB, tile), jnp.float32)

    def channel(c, sums):
        plane = left_ref[c].astype(jnp.float32)
        at = pl.ds(pl.multiple_of(c * SUB, SUB), SUB)
        lf[0, at, :] = plane[:, :LANES]
        lf[1, at, :] = plane[:, LANES:]
        return tuple(s + d for s, d in zip(sums, distances(plane)))

    per = CHANNEL_UNROLL

    def unrolled(body):
        def run(i, carry):
            for k in range(per):
                carry = body(i * per + k, carry)
            return carry

        return run

    weights = affinity(lax.fori_loop(0, channels // per, unrolled(channel), (zero,) * 5), channels)
    for i, k in enumerate(STEPS):
        w_ref[i] = weights[k]

    for q in range(channels // PER):
        planes = [
            (lf[0, (q * PER + s) * SUB : (q * PER + s + 1) * SUB, :],
             lf[1, (q * PER + s) * SUB : (q * PER + s + 1) * SUB, :])
            for s in range(PER)
        ]
        own[BLOCKS + q] = pack(planes)
    mask_at = BLOCKS + channels // PER
    own[mask_at] = pack([(usable[:, :LANES], usable[:, LANES:])] * PER)
    for q in range(mask_at + 1, own.shape[0]):
        own[q] = jnp.zeros((SUB, LANES), jnp.float32)

    @pl.when(has_left)
    def _():
        tile_copy.wait_recv()

    def shifts(c, carry):
        at = pl.ds(pl.multiple_of(c * SUB, SUB), SUB)
        before = prev[c].astype(jnp.float32)
        mine = right_ref[c].astype(jnp.float32)
        parts = (before[:, :LANES], before[:, LANES:], mine[:, :LANES], mine[:, LANES:])
        for s in range(4):
            rolled = [lroll(p, -s) for p in parts]
            for t in range(4):
                value = rolled[t]
                if s and t < 3:
                    value = jnp.where(lane < LANES - s, value, rolled[t + 1])
                rs[s, t, at, :] = value
        return carry

    lax.fori_loop(0, channels // per, unrolled(shifts), 0)

    depth = 8 * channels
    keep = (iota((depth, tile), 0) // channels == iota((depth, tile), 1) % 8).astype(jnp.bfloat16)
    rows_out = tile - 8 + D
    begin = tile - D + 1

    def row(i, carry):
        for h in range(ROW_UNROLL):
            y = i * ROW_UNROLL + h
            for t in range(4):
                block = jnp.concatenate(
                    [rs[s, t, pl.ds(y, channels, stride=SUB), :] for s in range(4)], axis=0
                )
                t4[h, t * LANES : (t + 1) * LANES, :] = block.T
        for h in range(ROW_UNROLL):
            y = i * ROW_UNROLL + h
            lhs = jnp.concatenate(
                [t4[h, begin : begin + rows_out, :], t4[h, begin + 4 : begin + 4 + rows_out, :]],
                axis=1,
            ).astype(jnp.bfloat16)
            l_row = jnp.concatenate(
                [lf[t, pl.ds(y, channels, stride=SUB), :] for t in range(2)], axis=1
            ).astype(jnp.bfloat16)
            rhs = jnp.concatenate([l_row] * 8, axis=0) * keep
            scores = jnp.dot(lhs, rhs, preferred_element_type=jnp.float32)
            for t in range(2):
                x = scores[LANES * t : LANES * t + D + LANES - 8, LANES * t : LANES * (t + 1)]
                for bit in (64, 32, 16, 8):
                    size = x.shape[0] - bit
                    on = (iota((size, LANES), 1) // bit) % 2 == 1
                    x = jnp.where(on, x[bit:], x[:size])
                u[t, pl.ds(pl.multiple_of(y * PITCH, 8), D), :] = x
        return carry

    lax.fori_loop(0, SUB // ROW_UNROLL, row, 0)

    scale = LOG2E / math.sqrt(channels)
    reach = offs_ref[0] * tile
    half = [usable[:, :LANES], usable[:, LANES:]]
    none = jnp.zeros((SUB, LANES), jnp.float32)
    for t in range(2):
        v[t, :SUB, :] = none
        v[t, (D + 1) * SUB :, :] = none
    st[:SUB, :] = none
    st[(BLOCKS + 1) * SUB :, :] = none

    def first(i, sums):
        sums = list(sums)
        for h in range(FIRST_UNROLL):
            b = i * FIRST_UNROLL + h
            planes = []
            for s in range(PER):
                j = b * PER + s
                pair = []
                for t in range(2):
                    corr = u[t, pl.ds(j, SUB, stride=PITCH), :] * scale
                    allowed = lane >= (D - 1 - j) - reach - t * LANES
                    value = jnp.where(allowed, corr, FLOOR_COST * LOG2E) * half[t]
                    v[t, pl.ds(pl.multiple_of((j + 1) * SUB, SUB), SUB), :] = value
                    e = jnp.exp2(value)
                    sums[2 * t] += e
                    sums[2 * t + 1] += e * e
                    pair.append(value)
                planes.append(pair)
            own[b] = pack(planes)
        return tuple(sums)

    sums = lax.fori_loop(0, BLOCKS // FIRST_UNROLL, first, (none,) * 4)

    place4 = (lane % GROUP) // 4
    for m in range(sent.shape[0]):
        out = own[4 * m]
        for s, (p, q) in ((1, (3, 0)), (2, (5, 2)), (3, (7, 4))):
            out = jnp.where((place4 == p) | (place4 == q), lroll(own[4 * m + s], 8 * s), out)
        sent[m] = out

    @pl.when(has_right)
    def _():
        strip_right.start()

    @pl.when(has_left)
    def _():
        strip_left.start()

    sums = lax.fori_loop(
        0, ITERS - 1, lambda i, s: step(v, st, w_ref, usable, None, s), sums
    )

    @pl.when(has_left)
    def _():
        strip_right.wait_recv()

    @pl.when(has_right)
    def _():
        strip_left.wait_recv()

    place = lane % GROUP

    def joined(m, s):
        out = jnp.where(place < 4, lroll(from_left[m], -24 - 8 * s), own[4 * m + s])
        return jnp.where(place >= 28, lroll(from_right[m], 24 - 8 * s), out)

    def over_groups(x):
        x = x + lroll(x, GROUP)
        return x + lroll(x, 2 * GROUP)

    s1, s2 = none, none
    for m in range(BLOCKS // 4):
        for s in range(4):
            value = joined(m, s)
            st[(4 * m + s + 1) * SUB : (4 * m + s + 2) * SUB, :] = value
            e = jnp.exp2(value)
            s1, s2 = s1 + e, s2 + e * e
    strip_sums = (none,) * 5
    for q in range(channels // PER):
        at = BLOCKS + q
        strip_sums = [
            a + d for a, d in zip(strip_sums, distances(joined(at // 4, at % 4)))
        ]
    strip_weights = affinity([over_groups(x) for x in strip_sums], channels)
    strip_usable = joined(mask_at // 4, mask_at % 4)
    low, high = lane < GROUP, lane >= LANES - GROUP

    def strip_step(i, sums):
        w, keep_own = coefficients(
            strip_weights, strip_usable, over_groups(sums[0]), over_groups(sums[1])
        )

        def pooled(ref, s):
            rows = three(ref, s)
            z = columns(w, *rows)
            p = z[1] + (lroll(z[0], 1) + lroll(z[2], -1))
            return p, lroll(p, GROUP), lroll(p, -GROUP), rows[1]

        def finish(b, p, up, before, down, after, value, acc):
            lower, upper = jnp.where(low, before, up), jnp.where(high, after, down)
            new = keep_own * value + ((lower + upper) + 2.0 * p)
            st[pl.ds(pl.multiple_of((b + 1) * SUB, SUB), SUB), :] = new
            e = jnp.exp2(new)
            return acc[0] + e, acc[1] + e * e

        def advance(ref, b, s, carry):
            p, up, down, before, value, acc = carry
            p_now, up_now, down_now, value_now = pooled(ref, s)
            acc = finish(b * STRIP_UNROLL + s - 1, p, up, before, down, down_now, value, acc)
            return p_now, up_now, down_now, up, value_now, acc

        def block_ref(b):
            at = pl.ds(pl.multiple_of(b * (STRIP_UNROLL * SUB), SUB), (STRIP_UNROLL + 2) * SUB)
            return st.at[at, :]

        def loop(b, carry):
            ref = block_ref(b)
            for k in range(STRIP_UNROLL):
                carry = advance(ref, b, k, carry)
            return carry

        ref = block_ref(0)
        p, up, down, value = pooled(ref, 0)
        carry = p, up, down, p, value, (none, none)
        for k in range(1, STRIP_UNROLL):
            carry = advance(ref, jnp.int32(0), k, carry)
        p, up, down, before, value, acc = lax.fori_loop(1, BLOCKS // STRIP_UNROLL, loop, carry)
        return finish(jnp.int32(BLOCKS - 1), p, up, before, down, p, value, acc)

    lax.fori_loop(0, ITERS, strip_step, (s1, s2))

    for t in range(4):
        sums_ref[t] = sums[t]

    @pl.when(has_right)
    def _():
        tile_copy.wait_send()
        strip_right.wait_send()

    @pl.when(has_left)
    def _():
        strip_left.wait_send()


def last_kernel(mask_ref, v, st, w_ref, sums_ref, disp_ref, vol_ref):
    usable = mask_ref[...].astype(jnp.float32)
    out = step(v, st, w_ref, usable, vol_ref, [sums_ref[t] for t in range(4)])
    for t in range(2):
        disp_ref[:, t * LANES : (t + 1) * LANES] = out[2 * t + 1] / out[2 * t]


def on_device(n, left_features, right_features, tile_offsets, valid_mask):
    channels, rows, tile = left_features.shape
    vmem = pl.BlockSpec(memory_space=pltpu.VMEM)
    strips = -(-(BLOCKS + channels // PER + 1) // 4) * 4
    f32 = jnp.float32
    state = pl.pallas_call(
        functools.partial(kernel, n),
        out_shape=(
            jax.ShapeDtypeStruct((2, (D + 2) * SUB, LANES), f32),
            jax.ShapeDtypeStruct(((BLOCKS + 2) * SUB, LANES), f32),
            jax.ShapeDtypeStruct((len(STEPS), SUB, tile), f32),
            jax.ShapeDtypeStruct((4, SUB, LANES), f32),
        ),
        in_specs=[vmem, vmem, pl.BlockSpec(memory_space=pltpu.SMEM), vmem],
        out_specs=(vmem,) * 4,
        scratch_shapes=[
            pltpu.VMEM((channels, rows, tile), jnp.bfloat16),
            pltpu.VMEM((2, channels * SUB, LANES), f32),
            pltpu.VMEM((4, 4, channels * SUB, LANES), f32),
            pltpu.VMEM((ROW_UNROLL, 2 * tile, LANES), f32),
            pltpu.VMEM((2, SUB * PITCH, LANES), f32),
            pltpu.VMEM((strips, SUB, LANES), f32),
            pltpu.VMEM((strips // 4, SUB, LANES), f32),
            pltpu.VMEM((strips // 4, SUB, LANES), f32),
            pltpu.VMEM((strips // 4, SUB, LANES), f32),
            pltpu.SemaphoreType.DMA((3,)),
            pltpu.SemaphoreType.DMA((3,)),
        ],
        compiler_params=pltpu.CompilerParams(
            collective_id=0, has_side_effects=True, vmem_limit_bytes=VMEM_LIMIT
        ),
    )(left_features, right_features, tile_offsets, valid_mask)
    return pl.pallas_call(
        last_kernel,
        out_shape=(
            jax.ShapeDtypeStruct((rows, tile), f32),
            jax.ShapeDtypeStruct((D, rows, tile), jnp.bfloat16),
        ),
        in_specs=[vmem] * 5,
        out_specs=(vmem, vmem),
        compiler_params=pltpu.CompilerParams(vmem_limit_bytes=VMEM_LIMIT),
    )(valid_mask, *state)


def solution(mesh):
    return jax.shard_map(
        functools.partial(on_device, mesh.shape["col"]),
        mesh=mesh,
        in_specs=(
            P(None, None, ("groups", "col")),
            P(None, None, ("groups", "col")),
            P(("groups", "col")),
            P(None, ("groups", "col")),
        ),
        out_specs=(P(None, ("groups", "col")), P(None, None, ("groups", "col"))),
        check_vma=False,
    )
```

```python
import functools
import math

import jax
import jax.numpy as jnp
from jax import lax
from jax.experimental import pallas as pl
from jax.experimental.pallas import tpu as pltpu
from jax.sharding import PartitionSpec as P

D = 192
ITERS = 4
FLOOR_COST = -4.0
LANES = 128
SUB = 8
MESH = pl.DeviceIdType.MESH
STEPS = tuple((a, b) for a in (-1, 0, 1) for b in (-1, 0, 1))
PITCH = D + 8
GROUP = 32
PER = LANES // GROUP
BLOCKS = D // PER
LOG2E = math.log2(math.e)
FIRST_UNROLL = 48
UNROLL = 192
STRIP_UNROLL = 48
ROW_UNROLL = 8
CHANNEL_UNROLL = 32
VMEM_LIMIT = 24 * 1024 * 1024


def lroll(x, shift):
    shift = shift % x.shape[-1]
    return x if shift == 0 else pltpu.roll(x, shift, x.ndim - 1)


def sroll(x, shift):
    shift = shift % x.shape[-2]
    return x if shift == 0 else pltpu.roll(x, shift, x.ndim - 2)


def iota(shape, dim):
    return lax.broadcasted_iota(jnp.int32, shape, dim)


def distances(plane):
    right = lroll(plane, -1)
    others = (right, sroll(plane, -1), sroll(right, -1), sroll(lroll(plane, 1), -1))
    return tuple((plane - other) ** 2 for other in others) + (plane * plane,)


def affinity(sums, channels):
    across, down, down_right, down_left, norm = sums
    row = iota(across.shape, 0)
    first, last = row == 0, row == across.shape[0] - 1
    dist = {(1, 0): across, (-1, 0): lroll(across, 1)}
    for a, base in ((1, down_right), (0, down), (-1, down_left)):
        dist[a, 1] = jnp.where(last, norm, base)
        dist[-a, -1] = jnp.where(first, norm, sroll(lroll(base, a), 1))
    e = {k: jnp.exp(-d / (2.0 * channels)) for k, d in dist.items()}
    e[0, 0] = jnp.ones_like(across)
    total = sum(e[k] for k in STEPS)
    out = {k: e[k] / total for k in STEPS}
    for a in (-1, 0, 1):
        out[a, 1] = jnp.where(last, 0.0, out[a, 1])
        out[a, -1] = jnp.where(first, 0.0, out[a, -1])
    return out


def coefficients(weights, usable, s1, s2):
    purity = D * s2 / (s1 * s1)
    gating = purity / (1.0 + purity)
    part = 0.25 * usable * (1.0 - gating)
    return {k: lroll(weights[k] * part, k[0]) for k in STEPS}, usable * gating


def columns(w, above, mid, below):
    return [w[a, -1] * above + w[a, 0] * mid + w[a, 1] * below for a in (-1, 0, 1)]


def three(ref, s):
    at = (s + 1) * SUB
    return ref[at - 1 : at - 1 + SUB, :], ref[at : at + SUB, :], ref[at + 1 : at + 1 + SUB, :]


def pack(planes):
    lane = iota((SUB, LANES), 1)
    place = lane % GROUP
    out = jnp.zeros((SUB, LANES), jnp.float32)
    for s, (head, tail) in enumerate(planes):
        mine = lane // GROUP == s
        out = jnp.where(mine & (place >= 4) & (place < 16), lroll(head, GROUP * s + 4), out)
        out = jnp.where(mine & (place >= 16) & (place < 28), lroll(tail, GROUP * s + 16 - 116), out)
    return out


def step(v, st, w_ref, usable, vol_ref, sums):
    last = vol_ref is not None
    lane = iota((SUB, LANES), 1)
    head_lane, tail_lane = lane == 0, lane == LANES - 1
    none = jnp.zeros((SUB, LANES), jnp.float32)
    wide = lambda a, b: jnp.concatenate([a, b], axis=1)
    w, keep_own = coefficients(
        {k: w_ref[i] for i, k in enumerate(STEPS)}, usable,
        wide(sums[0], sums[2]), wide(sums[1], sums[3]),
    )
    cut = lambda x, t: x[:, t * LANES : (t + 1) * LANES]
    w = [{k: cut(w[k], t) for k in STEPS} for t in range(2)]
    keep_own = [cut(keep_own, t) for t in range(2)]

    def pooled(refs, s):
        z, mid = [], []
        for t in range(2):
            rows = three(refs[t], s)
            mid.append(rows[1])
            z.append(columns(w[t], *rows))
        r = [lroll(z[t][0], 1) for t in range(2)]
        l = [lroll(z[t][2], -1) for t in range(2)]
        r[1] = jnp.where(head_lane, r[0], r[1])
        l[0] = jnp.where(tail_lane, l[1], l[0])
        return [z[t][1] + (r[t] + l[t]) for t in range(2)], mid

    def finish(b, s, pair, sums):
        j = b * UNROLL + s
        pair, sums = list(pair), list(sums)
        if last:
            group = s % PER
            row = pl.multiple_of((b * (UNROLL // PER) + s // PER + 1) * SUB, SUB)
            strip = st[pl.ds(row, SUB), :]
            pair[0] = jnp.where(lane < 4, lroll(strip, -(GROUP * group + 4)), pair[0])
            pair[1] = jnp.where(lane >= LANES - 4, lroll(strip, 100 - GROUP * group), pair[1])
            out = jnp.concatenate(pair, axis=1) * (1.0 / LOG2E)
            vol_ref[D - 1 - j] = out.astype(jnp.bfloat16)
            level = (D - 1 - j).astype(jnp.float32) * (1.0 / D)
        for t in range(2):
            if not last:
                v[t, pl.ds(pl.multiple_of((j + 1) * SUB, SUB), SUB), :] = pair[t]
            e = jnp.exp2(pair[t])
            sums[2 * t] += e
            sums[2 * t + 1] += e * (level if last else e)
        return sums

    def advance(refs, b, s, carry):
        p_prev, s_prev, v_prev, acc = carry
        p, mid = pooled(refs, s)
        s_now = [p_prev[t] + p[t] for t in range(2)]
        new = [keep_own[t] * v_prev[t] + (s_prev[t] + s_now[t]) for t in range(2)]
        before = (b - 1, UNROLL - 1) if s == 0 else (b, s - 1)
        return p, s_now, mid, finish(*before, new, acc)

    def block_refs(b):
        at = pl.ds(pl.multiple_of(b * (UNROLL * SUB), SUB), (UNROLL + 2) * SUB)
        return [v.at[t, at, :] for t in range(2)]

    def loop(b, carry):
        p, s, m, acc = carry
        carry = list(p), list(s), list(m), list(acc)
        refs = block_refs(b)
        for k in range(UNROLL):
            carry = advance(refs, b, k, carry)
        return tuple(tuple(c) for c in carry)

    refs = block_refs(0)
    p, mid = pooled(refs, 0)
    carry = p, [2.0 * x for x in p], mid, [none] * 4
    for k in range(1, UNROLL):
        carry = advance(refs, jnp.int32(0), k, carry)
    carry = tuple(tuple(c) for c in carry)
    p_prev, s_prev, v_prev, acc = lax.fori_loop(1, D // UNROLL, loop, carry)
    new = [keep_own[t] * v_prev[t] + (s_prev[t] + 2.0 * p_prev[t]) for t in range(2)]
    return tuple(finish(jnp.int32(D // UNROLL - 1), UNROLL - 1, new, acc))


def kernel(
    n, left_ref, right_ref, offs_ref, mask_ref, v, st, w_ref, sums_ref,
    prev, lf, rs, t4, u, own, sent, from_left, from_right, send_sem, recv_sem,
):
    channels = left_ref.shape[0]
    tile = left_ref.shape[2]
    me = lax.axis_index("col")
    has_left, has_right = me > 0, me < n - 1
    lane = iota((SUB, LANES), 1)

    barrier = pltpu.get_barrier_semaphore()

    @pl.when(has_left)
    def _():
        pl.semaphore_signal(barrier, inc=1, device_id={"col": me - 1}, device_id_type=MESH)

    @pl.when(has_right)
    def _():
        pl.semaphore_signal(barrier, inc=1, device_id={"col": me + 1}, device_id_type=MESH)

    pl.semaphore_wait(barrier, has_left.astype(jnp.int32) + has_right.astype(jnp.int32))

    def remote(src, dst, slot, to):
        return pltpu.make_async_remote_copy(
            src_ref=src, dst_ref=dst, send_sem=send_sem.at[slot], recv_sem=recv_sem.at[slot],
            device_id={"col": to}, device_id_type=MESH,
        )

    tile_copy = remote(right_ref, prev, 0, me + 1)
    strip_right = remote(sent, from_left, 1, me + 1)
    strip_left = remote(sent, from_right, 2, me - 1)

    @pl.when(has_right)
    def _():
        tile_copy.start()

    @pl.when(jnp.logical_not(has_left))
    def _():
        prev[...] = jnp.zeros(prev.shape, prev.dtype)
        from_left[...] = jnp.zeros(from_left.shape, jnp.float32)

    @pl.when(jnp.logical_not(has_right))
    def _():
        from_right[...] = jnp.zeros(from_right.shape, jnp.float32)

    usable = mask_ref[...].astype(jnp.float32)

    zero = jnp.zeros((SUB, tile), jnp.float32)

    def channel(c, sums):
        plane = left_ref[c].astype(jnp.float32)
        at = pl.ds(pl.multiple_of(c * SUB, SUB), SUB)
        lf[0, at, :] = plane[:, :LANES]
        lf[1, at, :] = plane[:, LANES:]
        return tuple(s + d for s, d in zip(sums, distances(plane)))

    per = CHANNEL_UNROLL

    def unrolled(body):
        def run(i, carry):
            for k in range(per):
                carry = body(i * per + k, carry)
            return carry

        return run

    weights = affinity(lax.fori_loop(0, channels // per, unrolled(channel), (zero,) * 5), channels)
    for i, k in enumerate(STEPS):
        w_ref[i] = weights[k]

    for q in range(channels // PER):
        planes = [
            (lf[0, (q * PER + s) * SUB : (q * PER + s + 1) * SUB, :],
             lf[1, (q * PER + s) * SUB : (q * PER + s + 1) * SUB, :])
            for s in range(PER)
        ]
        own[BLOCKS + q] = pack(planes)
    mask_at = BLOCKS + channels // PER
    own[mask_at] = pack([(usable[:, :LANES], usable[:, LANES:])] * PER)
    for q in range(mask_at + 1, own.shape[0]):
        own[q] = jnp.zeros((SUB, LANES), jnp.float32)

    @pl.when(has_left)
    def _():
        tile_copy.wait_recv()

    def shifts(c, carry):
        at = pl.ds(pl.multiple_of(c * SUB, SUB), SUB)
        before = prev[c].astype(jnp.float32)
        mine = right_ref[c].astype(jnp.float32)
        parts = (before[:, :LANES], before[:, LANES:], mine[:, :LANES], mine[:, LANES:])
        for s in range(4):
            rolled = [lroll(p, -s) for p in parts]
            for t in range(4):
                value = rolled[t]
                if s and t < 3:
                    value = jnp.where(lane < LANES - s, value, rolled[t + 1])
                rs[s, t, at, :] = value
        return carry

    lax.fori_loop(0, channels // per, unrolled(shifts), 0)

    depth = 8 * channels
    keep = (iota((depth, tile), 0) // channels == iota((depth, tile), 1) % 8).astype(jnp.bfloat16)
    rows_out = tile - 8 + D
    begin = tile - D + 1

    def row(i, carry):
        for h in range(ROW_UNROLL):
            y = i * ROW_UNROLL + h
            for t in range(4):
                block = jnp.concatenate(
                    [rs[s, t, pl.ds(y, channels, stride=SUB), :] for s in range(4)], axis=0
                )
                t4[h, t * LANES : (t + 1) * LANES, :] = block.T
        for h in range(ROW_UNROLL):
            y = i * ROW_UNROLL + h
            lhs = jnp.concatenate(
                [t4[h, begin : begin + rows_out, :], t4[h, begin + 4 : begin + 4 + rows_out, :]],
                axis=1,
            ).astype(jnp.bfloat16)
            l_row = jnp.concatenate(
                [lf[t, pl.ds(y, channels, stride=SUB), :] for t in range(2)], axis=1
            ).astype(jnp.bfloat16)
            rhs = jnp.concatenate([l_row] * 8, axis=0) * keep
            scores = jnp.dot(lhs, rhs, preferred_element_type=jnp.float32)
            for t in range(2):
                x = scores[LANES * t : LANES * t + D + LANES - 8, LANES * t : LANES * (t + 1)]
                for bit in (64, 32, 16, 8):
                    size = x.shape[0] - bit
                    on = (iota((size, LANES), 1) // bit) % 2 == 1
                    x = jnp.where(on, x[bit:], x[:size])
                u[t, pl.ds(pl.multiple_of(y * PITCH, 8), D), :] = x
        return carry

    lax.fori_loop(0, SUB // ROW_UNROLL, row, 0)

    scale = LOG2E / math.sqrt(channels)
    reach = offs_ref[0] * tile
    half = [usable[:, :LANES], usable[:, LANES:]]
    none = jnp.zeros((SUB, LANES), jnp.float32)
    for t in range(2):
        v[t, :SUB, :] = none
        v[t, (D + 1) * SUB :, :] = none
    st[:SUB, :] = none
    st[(BLOCKS + 1) * SUB :, :] = none

    def first(i, sums):
        sums = list(sums)
        for h in range(FIRST_UNROLL):
            b = i * FIRST_UNROLL + h
            planes = []
            for s in range(PER):
                j = b * PER + s
                pair = []
                for t in range(2):
                    corr = u[t, pl.ds(j, SUB, stride=PITCH), :] * scale
                    allowed = lane >= (D - 1 - j) - reach - t * LANES
                    value = jnp.where(allowed, corr, FLOOR_COST * LOG2E) * half[t]
                    v[t, pl.ds(pl.multiple_of((j + 1) * SUB, SUB), SUB), :] = value
                    e = jnp.exp2(value)
                    sums[2 * t] += e
                    sums[2 * t + 1] += e * e
                    pair.append(value)
                planes.append(pair)
            own[b] = pack(planes)
        return tuple(sums)

    sums = lax.fori_loop(0, BLOCKS // FIRST_UNROLL, first, (none,) * 4)

    place4 = (lane % GROUP) // 4
    for m in range(sent.shape[0]):
        out = own[4 * m]
        for s, (p, q) in ((1, (3, 0)), (2, (5, 2)), (3, (7, 4))):
            out = jnp.where((place4 == p) | (place4 == q), lroll(own[4 * m + s], 8 * s), out)
        sent[m] = out

    @pl.when(has_right)
    def _():
        strip_right.start()

    @pl.when(has_left)
    def _():
        strip_left.start()

    sums = lax.fori_loop(
        0, ITERS - 1, lambda i, s: step(v, st, w_ref, usable, None, s), sums
    )

    @pl.when(has_left)
    def _():
        strip_right.wait_recv()

    @pl.when(has_right)
    def _():
        strip_left.wait_recv()

    place = lane % GROUP

    def joined(m, s):
        out = jnp.where(place < 4, lroll(from_left[m], -24 - 8 * s), own[4 * m + s])
        return jnp.where(place >= 28, lroll(from_right[m], 24 - 8 * s), out)

    def over_groups(x):
        x = x + lroll(x, GROUP)
        return x + lroll(x, 2 * GROUP)

    s1, s2 = none, none
    for m in range(BLOCKS // 4):
        for s in range(4):
            value = joined(m, s)
            st[(4 * m + s + 1) * SUB : (4 * m + s + 2) * SUB, :] = value
            e = jnp.exp2(value)
            s1, s2 = s1 + e, s2 + e * e
    strip_sums = (none,) * 5
    for q in range(channels // PER):
        at = BLOCKS + q
        strip_sums = [
            a + d for a, d in zip(strip_sums, distances(joined(at // 4, at % 4)))
        ]
    strip_weights = affinity([over_groups(x) for x in strip_sums], channels)
    strip_usable = joined(mask_at // 4, mask_at % 4)
    low, high = lane < GROUP, lane >= LANES - GROUP

    def strip_step(i, sums):
        w, keep_own = coefficients(
            strip_weights, strip_usable, over_groups(sums[0]), over_groups(sums[1])
        )

        def pooled(ref, s):
            rows = three(ref, s)
            z = columns(w, *rows)
            p = z[1] + (lroll(z[0], 1) + lroll(z[2], -1))
            return p, lroll(p, GROUP), lroll(p, -GROUP), rows[1]

        def finish(b, p, up, before, down, after, value, acc):
            lower, upper = jnp.where(low, before, up), jnp.where(high, after, down)
            new = keep_own * value + ((lower + upper) + 2.0 * p)
            st[pl.ds(pl.multiple_of((b + 1) * SUB, SUB), SUB), :] = new
            e = jnp.exp2(new)
            return acc[0] + e, acc[1] + e * e

        def advance(ref, b, s, carry):
            p, up, down, before, value, acc = carry
            p_now, up_now, down_now, value_now = pooled(ref, s)
            acc = finish(b * STRIP_UNROLL + s - 1, p, up, before, down, down_now, value, acc)
            return p_now, up_now, down_now, up, value_now, acc

        def block_ref(b):
            at = pl.ds(pl.multiple_of(b * (STRIP_UNROLL * SUB), SUB), (STRIP_UNROLL + 2) * SUB)
            return st.at[at, :]

        def loop(b, carry):
            ref = block_ref(b)
            for k in range(STRIP_UNROLL):
                carry = advance(ref, b, k, carry)
            return carry

        ref = block_ref(0)
        p, up, down, value = pooled(ref, 0)
        carry = p, up, down, p, value, (none, none)
        for k in range(1, STRIP_UNROLL):
            carry = advance(ref, jnp.int32(0), k, carry)
        p, up, down, before, value, acc = lax.fori_loop(1, BLOCKS // STRIP_UNROLL, loop, carry)
        return finish(jnp.int32(BLOCKS - 1), p, up, before, down, p, value, acc)

    lax.fori_loop(0, ITERS, strip_step, (s1, s2))

    for t in range(4):
        sums_ref[t] = sums[t]

    @pl.when(has_right)
    def _():
        tile_copy.wait_send()
        strip_right.wait_send()

    @pl.when(has_left)
    def _():
        strip_left.wait_send()


def last_kernel(mask_ref, v, st, w_ref, sums_ref, disp_ref, vol_ref):
    usable = mask_ref[...].astype(jnp.float32)
    out = step(v, st, w_ref, usable, vol_ref, [sums_ref[t] for t in range(4)])
    for t in range(2):
        disp_ref[:, t * LANES : (t + 1) * LANES] = out[2 * t + 1] / out[2 * t]


def on_device(n, left_features, right_features, tile_offsets, valid_mask):
    channels, rows, tile = left_features.shape
    vmem = pl.BlockSpec(memory_space=pltpu.VMEM)
    strips = -(-(BLOCKS + channels // PER + 1) // 4) * 4
    f32 = jnp.float32
    state = pl.pallas_call(
        functools.partial(kernel, n),
        out_shape=(
            jax.ShapeDtypeStruct((2, (D + 2) * SUB, LANES), f32),
            jax.ShapeDtypeStruct(((BLOCKS + 2) * SUB, LANES), f32),
            jax.ShapeDtypeStruct((len(STEPS), SUB, tile), f32),
            jax.ShapeDtypeStruct((4, SUB, LANES), f32),
        ),
        in_specs=[vmem, vmem, pl.BlockSpec(memory_space=pltpu.SMEM), vmem],
        out_specs=(vmem,) * 4,
        scratch_shapes=[
            pltpu.VMEM((channels, rows, tile), jnp.bfloat16),
            pltpu.VMEM((2, channels * SUB, LANES), f32),
            pltpu.VMEM((4, 4, channels * SUB, LANES), f32),
            pltpu.VMEM((ROW_UNROLL, 2 * tile, LANES), f32),
            pltpu.VMEM((2, SUB * PITCH, LANES), f32),
            pltpu.VMEM((strips, SUB, LANES), f32),
            pltpu.VMEM((strips // 4, SUB, LANES), f32),
            pltpu.VMEM((strips // 4, SUB, LANES), f32),
            pltpu.VMEM((strips // 4, SUB, LANES), f32),
            pltpu.SemaphoreType.DMA((3,)),
            pltpu.SemaphoreType.DMA((3,)),
        ],
        compiler_params=pltpu.CompilerParams(
            collective_id=0, has_side_effects=True, vmem_limit_bytes=VMEM_LIMIT
        ),
    )(left_features, right_features, tile_offsets, valid_mask)
    return pl.pallas_call(
        last_kernel,
        out_shape=(
            jax.ShapeDtypeStruct((rows, tile), f32),
            jax.ShapeDtypeStruct((D, rows, tile), jnp.bfloat16),
        ),
        in_specs=[vmem] * 5,
        out_specs=(vmem, vmem),
        compiler_params=pltpu.CompilerParams(vmem_limit_bytes=VMEM_LIMIT),
    )(valid_mask, *state)


def solution(mesh):
    return jax.shard_map(
        functools.partial(on_device, mesh.shape["col"]),
        mesh=mesh,
        in_specs=(
            P(None, None, ("groups", "col")),
            P(None, None, ("groups", "col")),
            P(("groups", "col")),
            P(None, ("groups", "col")),
        ),
        out_specs=(P(None, ("groups", "col")), P(None, None, ("groups", "col"))),
        check_vma=False,
    )
```
